32 devices in a mesh: grp: 16 (over z, x, core), mem: 2 (over y).
Axes of the slice: x: 2, y: 2, z: 4, core: 2. Of those that a mesh axis runs over, the one named last changes fastest.
Arguments:
- forcing: float32 [16, 256, 32, 128], P(None, 'grp', 'mem'), may hold values from -8 to 8
- aggregate: int32 [64, 8, 32], P('grp', 'mem'), may hold values from 0 to 8191, as said below
- factors: float32 [64, 128, 128], P('mem'), may hold values from -1.5 to 1.5, as said below
Outputs:
- solution: float32 [16, 256, 32, 128], P(None, 'grp', 'mem')
The draws below stay inside these ranges and needn't reach their ends.
Inputs may be any that keep to these rules, and one draw needn't show every extreme that they name: Coarse unknowns are numbered over the fine blocks with the first block index taken modulo half the number of blocks along the first dimension, consecutive numbers lying close together in the other dimensions, so that an aggregate joins blocks of both halves of the grid; a few blocks take the entry of a block beside them. `factors`: each of the 64 blocks is lower triangular with its diagonal between 0.5 and 1.5.
All inputs are finite; a program needn't handle non-finite values.
Results may differ from the reference program's by a relative error of at most 0.00013.
Values sent between devices are 32-bit elements; how exact they have to be, the bound alone decides.
A program may use at most 128 MiB of HBM per device.

```python
import math
import jax
import jax.numpy as jnp
from jax import lax

RHS = 16
NC = 8192
BS = 128
PRE = 3
POST = 2
NB = 64
NX = 256
NY = 32
NZ = 128


def draw_forcing(key, part):
    noise_key = jax.random.fold_in(jax.random.fold_in(key, 11), 0)
    base_noise = jax.random.normal(noise_key, (RHS, NX, NY, NZ), jnp.float32)
    values = base_noise
    return jnp.clip(values, -8.0, 8.0)


def draw_aggregate(key, part):
    blk_x = NX // 4
    blk_y = NY // 4
    blk_z = NZ // 4
    fold_x = blk_x // 2
    total = fold_x * blk_y * blk_z
    shape = (blk_x, blk_y, blk_z)
    linear = lax.broadcasted_iota(jnp.int32, shape, 0) % fold_x * (blk_y * blk_z) + lax.broadcasted_iota(jnp.int32, shape, 1) * blk_z + lax.broadcasted_iota(jnp.int32, shape, 2)
    if total >= NC:
        base = linear // (total // NC)
    else:
        base = linear * (NC // total)
    x_next = jnp.concatenate([base[1:], base[-1:]], axis=0)
    x_prev = jnp.concatenate([base[:1], base[:-1]], axis=0)
    y_next = jnp.concatenate([base[:, 1:], base[:, -1:]], axis=1)
    y_prev = jnp.concatenate([base[:, :1], base[:, :-1]], axis=1)
    picks = jax.random.randint(jax.random.fold_in(key, 37), shape, 0, 24)
    moved = jnp.where(picks == 0, x_next, jnp.where(picks == 1, x_prev, jnp.where(picks == 2, y_next, jnp.where(picks == 3, y_prev, base))))
    return moved.astype(jnp.int32)


def draw_factors(key, part):
    first_key, second_key = jax.random.split(jax.random.fold_in(key, 23))
    lower = jnp.clip(jax.random.normal(first_key, (NB, BS, BS), jnp.float32) * (0.5 / math.sqrt(BS)), -1.5, 1.5)
    diag_vals = jax.random.uniform(second_key, (NB, BS), jnp.float32, 0.5, 1.5)
    row_ids = lax.broadcasted_iota(jnp.int32, (BS, BS), 0)
    col_ids = lax.broadcasted_iota(jnp.int32, (BS, BS), 1)
    strict = jnp.where(row_ids > col_ids, lower, 0.0)
    return strict + jnp.where(row_ids == col_ids, diag_vals[:, :, None], 0.0)


def setup_inputs(seed: int = 0) -> dict:
    streams_of = jax.random.split(jax.random.key(seed), 4)
    forcing = draw_forcing(jax.random.fold_in(streams_of[3], 71), 0)
    aggregate = draw_aggregate(jax.random.fold_in(streams_of[3], 71), 0)
    factors = draw_factors(jax.random.fold_in(streams_of[3], 71), 0)
    return {"forcing": forcing, "aggregate": aggregate, "factors": factors}


relaxation = 0.8


def apply_operator(values):
    padded = jnp.pad(values, 1)
    beside = padded[2:, 1:-1, 1:-1] + padded[:-2, 1:-1, 1:-1]
    beside = beside + padded[1:-1, 2:, 1:-1] + padded[1:-1, :-2, 1:-1]
    beside = beside + padded[1:-1, 1:-1, 2:] + padded[1:-1, 1:-1, :-2]
    return 6.0 * values - beside


def restrict_blocks(residual, aggregate):
    blk_x, blk_y, blk_z = aggregate.shape
    means = residual.reshape(blk_x, 4, blk_y, 4, blk_z, 4).mean(axis=(1, 3, 5))
    return jax.ops.segment_sum(means.reshape(-1), aggregate.reshape(-1), num_segments=NC)


def prolong_blocks(coarse_fix, aggregate):
    blk_x, blk_y, blk_z = aggregate.shape
    picked = jnp.take(coarse_fix, aggregate.reshape(-1)).reshape(blk_x, 1, blk_y, 1, blk_z, 1)
    return jnp.broadcast_to(picked, (blk_x, 4, blk_y, 4, blk_z, 4)).reshape(blk_x * 4, blk_y * 4, blk_z * 4)


def reference(forcing, aggregate, factors):
    weight = relaxation / 6.0

    def one_side(source):
        smoothed = weight * source
        for repeat in range(PRE - 1):
            smoothed = smoothed + weight * (source - apply_operator(smoothed))
        residual = source - apply_operator(smoothed)
        coarse_rhs = restrict_blocks(residual, aggregate).reshape(NB, BS)
        inner = jnp.einsum('bij,bj->bi', factors, coarse_rhs, precision=lax.Precision.HIGHEST)
        coarse_fix = jnp.einsum('bij,bi->bj', factors, inner, precision=lax.Precision.HIGHEST).reshape(NC)
        lifted = prolong_blocks(coarse_fix, aggregate)
        solution = smoothed + (lifted - weight * apply_operator(lifted))
        for repeat in range(POST):
            solution = solution + weight * (source - apply_operator(solution))
        return solution

    return lax.map(one_side, forcing)
```

```python
import functools

import jax
import jax.numpy as jnp
from jax import lax
from jax.experimental import pallas as pl
from jax.experimental.pallas import tpu as pltpu
from jax.sharding import PartitionSpec as P

NC = 8192
relaxation = 0.8
WEIGHT = relaxation / 6.0
CELL = 4
HALO = 4
F32 = jnp.float32
BF16 = jnp.bfloat16
MESH = pl.DeviceIdType.MESH
VMEM = pltpu.VMEM


def vmem_spec():
    return pl.BlockSpec(memory_space=pltpu.VMEM)


def params(**kw):
    return pltpu.CompilerParams(vmem_limit_bytes=60 * 1024 * 1024, **kw)


def pieces(value):
    hi = value.astype(BF16)
    rest = value - hi.astype(F32)
    mid = rest.astype(BF16)
    low = (rest - mid.astype(F32)).astype(BF16)
    return jnp.concatenate([hi, mid, low], axis=0)


def joined(value):
    k = value.shape[0] // 3
    return value[:k] + (value[k : 2 * k] + value[2 * k :])


def halo_kernel(G, M, f_ref, a_ref, fe, ae, sx, rx, sy, ry):
    K, X, Y, Z = f_ref.shape
    bx, by = X // CELL, Y // CELL
    g, m = lax.axis_index("grp"), lax.axis_index("mem")
    flat = f_ref.reshape(K * X * Y, Z)

    sides = []
    if G > 1:
        sides += [(g > 0, {"grp": g - 1}), (g < G - 1, {"grp": g + 1})]
    if M > 1:
        sides += [(m > 0, {"mem": m - 1}), (m < M - 1, {"mem": m + 1})]
    barrier = pltpu.get_barrier_semaphore()
    for there, dev in sides:

        @pl.when(there)
        def _(dev=dev):
            pl.semaphore_signal(barrier, inc=1, device_id=dev, device_id_type=MESH)

    @pl.loop(0, X)
    def _(x):
        for y in range(Y):
            fe[HALO + x, HALO + y] = flat[pl.ds(x * Y + y, K, stride=X * Y), :]

    ae[1 : 1 + bx, 1 : 1 + by] = a_ref[...]

    def blank(start):
        @pl.loop(start, start + HALO)
        def _(x):
            fe[x, HALO : HALO + Y] = jnp.zeros((Y,) + fe.shape[2:], F32)

    @pl.when(g == 0)
    def _():
        blank(0)
        ae[0:1, 1 : 1 + by] = jnp.zeros((1, by) + ae.shape[2:], jnp.int32)

    @pl.when(g == G - 1)
    def _():
        blank(HALO + X)
        ae[1 + bx :, 1 : 1 + by] = jnp.zeros((1, by) + ae.shape[2:], jnp.int32)

    @pl.when(m == 0)
    def _():
        @pl.loop(0, X + 2 * HALO)
        def _(x):
            fe[x, 0:HALO] = jnp.zeros((HALO,) + fe.shape[2:], F32)

        ae[:, 0:1] = jnp.zeros((bx + 2, 1) + ae.shape[2:], jnp.int32)

    @pl.when(m == M - 1)
    def _():
        @pl.loop(0, X + 2 * HALO)
        def _(x):
            fe[x, HALO + Y :] = jnp.zeros((HALO,) + fe.shape[2:], F32)

        ae[:, 1 + by :] = jnp.zeros((bx + 2, 1) + ae.shape[2:], jnp.int32)

    def beside(index, count):
        return (index + count - 1) // count + (2 * (count - 1) - index) // count

    pl.semaphore_wait(barrier, beside(g, G) + beside(m, M))

    def copies(ref, h, n, axis, dev, send, recv, down, slot):
        def cut(start, length):
            if axis == 0:
                inner = ref.shape[1] - 2 * h
                return ref.at[pl.ds(start, length), pl.ds(h, inner)]
            return ref.at[:, pl.ds(start, length)]

        src = cut(h, h) if down else cut(n, h)
        dst = cut(n + h, h) if down else cut(0, h)
        return pltpu.make_async_remote_copy(
            src_ref=src,
            dst_ref=dst,
            send_sem=send.at[slot],
            recv_sem=recv.at[slot],
            device_id=dev,
            device_id_type=MESH,
        )

    def phase(axis, name, index, count, send, recv):
        if count == 1:
            return
        lower, upper = {name: index - 1}, {name: index + 1}
        nf, na = (X, bx) if axis == 0 else (Y, by)

        def make(down, dev):
            base = 0 if down else 2
            return (
                copies(fe, HALO, nf, axis, dev, send, recv, down, base),
                copies(ae, 1, na, axis, dev, send, recv, down, base + 1),
            )

        @pl.when(index > 0)
        def _():
            for c in make(True, lower):
                c.start()

        @pl.when(index < count - 1)
        def _():
            for c in make(False, upper):
                c.start()

        @pl.when(index > 0)
        def _():
            for c in make(True, lower):
                c.wait_send()
            for c in make(False, lower):
                c.wait_recv()

        @pl.when(index < count - 1)
        def _():
            for c in make(False, upper):
                c.wait_send()
            for c in make(True, upper):
                c.wait_recv()

    phase(0, "grp", g, G, sx, rx)
    phase(1, "mem", m, M, sy, ry)


def sweep(src, x0, x1, y0, y1, emit):
    Z = src.shape[-1]
    lane = lax.broadcasted_iota(jnp.int32, (src.shape[2], Z), 1)
    first, last = lane == 0, lane == Z - 1

    @pl.loop(x0, x1)
    def _(x):
        prev, here = src[x, y0 - 1], src[x, y0]
        for y in range(y0, y1):
            after = src[x, y + 1]
            near = src[x - 1, y] + src[x + 1, y] + (prev + after)
            low = jnp.where(first, 0.0, pltpu.roll(here, 1, 1))
            high = jnp.where(last, 0.0, pltpu.roll(here, Z - 1, 1))
            emit(x, y, here, near + (low + high))
            prev, here = here, after


def clear_outside(ref, G, M, X, Y, width):
    g, m = lax.axis_index("grp"), lax.axis_index("mem")
    h = HALO
    rest = ref.shape[2:]

    def rows(start):
        @pl.loop(start, start + width)
        def _(x):
            ref[x] = jnp.zeros(ref.shape[1:], F32)

    def columns(start):
        @pl.loop(h - width, h + X + width)
        def _(x):
            ref[x, start : start + width] = jnp.zeros((width,) + rest, F32)

    pl.when(g == 0)(lambda: rows(h - width))
    pl.when(g == G - 1)(lambda: rows(h + X))
    pl.when(m == 0)(lambda: columns(h - width))
    pl.when(m == M - 1)(lambda: columns(h + Y))


def pre_kernel(G, M, chunk, fe, ids_ref, s3, d_ref, s2, means):
    Xe, Ye, K, Z = fe.shape
    X, Y = Xe - 2 * HALO, Ye - 2 * HALO
    bx, by, bz = X // CELL, Y // CELL, Z // CELL
    w = WEIGHT

    def second(x, y, c, near):
        s2[x, y] = w * ((2.0 - 6.0 * w) * c + w * near)

    sweep(fe, 1, Xe - 1, 1, Ye - 1, second)
    clear_outside(s2, G, M, X, Y, 3)

    def third(x, y, c, near):
        s3[x, y] = (1.0 - 6.0 * w) * c + w * (fe[x, y] + near)

    sweep(s2, 2, Xe - 2, 2, Ye - 2, third)
    clear_outside(s3, G, M, X, Y, 2)

    def residual(x, y, c, near):
        s2[x, y] = fe[x, y] - 6.0 * c + near

    sweep(s3, HALO, HALO + X, HALO, HALO + Y, residual)

    rows = lax.broadcasted_iota(jnp.int32, (by * Z, by * bz), 0)
    cols = lax.broadcasted_iota(jnp.int32, (by * Z, by * bz), 1)
    spread = jnp.where(rows // CELL == cols, 1.0 / CELL**3, 0.0).astype(BF16)
    for i in range(bx):
        parts = []
        for j in range(by):
            total = None
            for p in range(CELL):
                for q in range(CELL):
                    v = s2[HALO + i * CELL + p, HALO + j * CELL + q]
                    total = v if total is None else total + v
            parts.append(total)
        line = jnp.concatenate(parts, axis=1)
        means[:, i * by * bz : (i + 1) * by * bz] = joined(
            jnp.dot(pieces(line), spread, preferred_element_type=F32)
        )
    split = pieces(means[...])
    ids = ids_ref[...]
    count = bx * by * bz

    @pl.loop(0, d_ref.shape[0])
    def _(o):
        entry = lax.broadcasted_iota(jnp.int32, (chunk, count), 0) + o * chunk
        hot = jnp.where(entry == ids, 1.0, 0.0).astype(BF16)
        got = lax.dot_general(
            split, hot, (((1,), (1,)), ((), ())), preferred_element_type=F32
        )
        d_ref[o] = joined(got)


def coarse_kernel(G, M, n_own, d_ref, fac_ref, x_ref, r, ssend, srecv, gsend, grecv):
    n = G * M
    owners = n_own * M
    g, m = lax.axis_index("grp"), lax.axis_index("mem")
    me = g * M + m
    own = m * n_own + g
    q, bs = fac_ref.shape[0], fac_ref.shape[1]
    everyone = n_own == G

    def device(i):
        return {"grp": i // M, "mem": i % M}

    def peer(t):
        return lax.rem(me + t, n)

    barrier = pltpu.get_barrier_semaphore()

    @pl.loop(1, n)
    def _(t):
        pl.semaphore_signal(barrier, inc=1, device_id=device(peer(t)), device_id_type=MESH)

    pl.semaphore_wait(barrier, n - 1)

    def owning(i, body):
        if everyone:
            body()
        else:
            pl.when(i // M < n_own)(body)

    @pl.loop(1, n)
    def _(t):
        to = peer(t)

        def go():
            pltpu.make_async_remote_copy(
                src_ref=d_ref.at[(to % M) * n_own + to // M],
                dst_ref=r.at[me],
                send_sem=ssend,
                recv_sem=srecv,
                device_id=device(to),
                device_id_type=MESH,
            ).start()

        owning(to, go)

    def wait_bytes(ref, count, sem):
        if count > 0:
            part = ref.at[pl.ds(0, count)]
            pltpu.make_async_copy(part, part, sem).wait()

    def solve():
        wait_bytes(r, n - 1, srecv)

        def add(t, total):
            return total + r[peer(t)]

        total = lax.fori_loop(1, n, add, d_ref[own])
        for b in range(q):
            rhs = total[:, b * bs : (b + 1) * bs]
            inner = lax.dot_general(
                rhs,
                fac_ref[b],
                (((1,), (1,)), ((), ())),
                precision=lax.Precision.HIGHEST,
                preferred_element_type=F32,
            )
            x_ref[own, :, b * bs : (b + 1) * bs] = lax.dot_general(
                inner,
                fac_ref[b],
                (((1,), (0,)), ((), ())),
                precision=lax.Precision.HIGHEST,
                preferred_element_type=F32,
            )

        @pl.loop(1, n)
        def _(t):
            pltpu.make_async_remote_copy(
                src_ref=x_ref.at[own],
                dst_ref=x_ref.at[own],
                send_sem=gsend,
                recv_sem=grecv,
                device_id=device(peer(t)),
                device_id_type=MESH,
            ).start()

    owning(me, solve)

    if everyone:
        wait_bytes(d_ref, n - 1, ssend)
        wait_bytes(x_ref, n - 1, grecv)
        wait_bytes(r, n - 1, gsend)
    else:
        mine = g < n_own

        @pl.when(mine)
        def _():
            wait_bytes(d_ref, owners - 1, ssend)
            wait_bytes(x_ref, owners - 1, grecv)
            wait_bytes(r, n - 1, gsend)

        @pl.when(jnp.logical_not(mine))
        def _():
            wait_bytes(d_ref, owners, ssend)
            wait_bytes(x_ref, owners, grecv)


def post_kernel(G, M, bs, fe, s3, ae, x_ref, o_ref, lifted, sol):
    Xe, Ye, K, Z = fe.shape
    X, Y = Xe - 2 * HALO, Ye - 2 * HALO
    bx, by, bz = X // CELL + 2, Y // CELL + 2, Z // CELL
    w = WEIGHT
    half = 8
    owners, q = x_ref.shape[0], x_ref.shape[2] // bs
    per = Z // bz
    groups = [range(s, min(s + per, by)) for s in range(0, by, per)]
    lane = lax.broadcasted_iota(jnp.int32, (half, Z), 1)

    def pick(table, index):
        return jnp.take_along_axis(table, index, axis=1)

    def line(i):
        for group in groups:
            index = None
            for slot, j in enumerate(group):
                packed = pick(ae[i, j], (lane % bz) * CELL)
                index = packed if index is None else jnp.where(lane // bz == slot, packed, index)
            inner = index % bs
            outer = index // bs
            found = [jnp.zeros((half, Z), F32) for _ in range(K // half)]

            def body(o, found):
                out = list(found)
                for b in range(q):
                    hit = outer == o * q + b
                    for h in range(K // half):
                        table = x_ref[o, h * half : (h + 1) * half, b * bs : (b + 1) * bs]
                        out[h] = jnp.where(hit, pick(table, inner), out[h])
                return tuple(out)

            found = lax.fori_loop(0, owners, body, tuple(found))
            for slot, j in enumerate(group):
                wide = [pick(v, lane // CELL + slot * bz) for v in found]
                value = jnp.concatenate(wide, axis=0)
                for p in range(CELL):
                    for r in range(CELL):
                        lifted[i * CELL + p, j * CELL + r] = value

    @pl.loop(0, bx)
    def _(i):
        line(i)

    clear_outside(lifted, G, M, X, Y, HALO)

    def start(x, y, c, near):
        sol[x, y] = s3[x, y] + ((1.0 - 6.0 * w) * c + w * near)

    sweep(lifted, 2, Xe - 2, 2, Ye - 2, start)
    clear_outside(sol, G, M, X, Y, 2)

    def first(x, y, c, near):
        lifted[x, y] = (1.0 - 6.0 * w) * c + w * (fe[x, y] + near)

    sweep(sol, 3, Xe - 3, 3, Ye - 3, first)
    clear_outside(lifted, G, M, X, Y, 1)

    flat = o_ref.reshape(K * X * Y, Z)

    def last(x, y, c, near):
        flat[pl.ds((x - HALO) * Y + (y - HALO), K, stride=X * Y), :] = (
            1.0 - 6.0 * w
        ) * c + w * (fe[x, y] + near)

    sweep(lifted, HALO, HALO + X, HALO, HALO + Y, last)


def shards(G, M, forcing, aggregate, factors):
    K, X, Y, Z = forcing.shape
    bx, by, bz = aggregate.shape
    Xe, Ye = X + 2 * HALO, Y + 2 * HALO
    local_blocks, bs = factors.shape[0], factors.shape[1]
    q = -(-local_blocks // G)
    n_own = local_blocks // q
    chunk = q * bs
    owners = n_own * M
    sd = jax.ShapeDtypeStruct

    wide_ids = jnp.broadcast_to(
        jnp.repeat(aggregate, CELL, axis=2)[:, :, None, :], (bx, by, 8, Z)
    )
    fe, ae = pl.pallas_call(
        functools.partial(halo_kernel, G, M),
        out_shape=(sd((Xe, Ye, K, Z), F32), sd((bx + 2, by + 2, 8, Z), jnp.int32)),
        in_specs=[vmem_spec()] * 2,
        out_specs=(vmem_spec(),) * 2,
        scratch_shapes=[pltpu.SemaphoreType.DMA((4,))] * 4,
        compiler_params=params(collective_id=0, has_side_effects=True),
        name="halo",
    )(forcing, wide_ids)

    s3, dense = pl.pallas_call(
        functools.partial(pre_kernel, G, M, chunk),
        out_shape=(sd((Xe, Ye, K, Z), F32), sd((owners, K, chunk), F32)),
        in_specs=[vmem_spec()] * 2,
        out_specs=(vmem_spec(),) * 2,
        scratch_shapes=[VMEM((Xe, Ye, K, Z), F32), VMEM((K, bx * by * bz), F32)],
        compiler_params=params(),
        name="pre",
    )(fe, aggregate.reshape(1, -1))

    g = lax.axis_index("grp")
    mine = lax.dynamic_slice_in_dim(factors, jnp.minimum(g, n_own - 1) * q, q, axis=0)
    fix = pl.pallas_call(
        functools.partial(coarse_kernel, G, M, n_own),
        out_shape=sd((owners, K, chunk), F32),
        in_specs=[vmem_spec()] * 2,
        out_specs=vmem_spec(),
        scratch_shapes=[VMEM((G * M, K, chunk), F32)] + [pltpu.SemaphoreType.DMA] * 4,
        compiler_params=params(collective_id=1, has_side_effects=True),
        name="coarse",
    )(dense, mine)

    return pl.pallas_call(
        functools.partial(post_kernel, G, M, bs),
        out_shape=sd((K, X, Y, Z), F32),
        in_specs=[vmem_spec()] * 4,
        out_specs=vmem_spec(),
        scratch_shapes=[VMEM((Xe, Ye, K, Z), F32)] * 2,
        compiler_params=params(),
        name="post",
    )(fe, s3, ae, fix)


def solution(mesh):
    placed = (P(None, "grp", "mem", None), P("grp", "mem", None), P("mem", None, None))
    body = functools.partial(shards, mesh.shape["grp"], mesh.shape["mem"])
    return jax.shard_map(
        body, mesh=mesh, in_specs=placed, out_specs=P(None, "grp", "mem", None), check_vma=False
    )
```

```python
import functools

import jax
import jax.numpy as jnp
from jax import lax
from jax.experimental import pallas as pl
from jax.experimental.pallas import tpu as pltpu
from jax.sharding import PartitionSpec as P

NC = 8192
relaxation = 0.8
WEIGHT = relaxation / 6.0
CELL = 4
HALO = 4
F32 = jnp.float32
BF16 = jnp.bfloat16
MESH = pl.DeviceIdType.MESH
VMEM = pltpu.VMEM


def vmem_spec():
    return pl.BlockSpec(memory_space=pltpu.VMEM)


def params(**kw):
    return pltpu.CompilerParams(vmem_limit_bytes=60 * 1024 * 1024, **kw)


def pieces(value):
    hi = value.astype(BF16)
    rest = value - hi.astype(F32)
    mid = rest.astype(BF16)
    low = (rest - mid.astype(F32)).astype(BF16)
    return jnp.concatenate([hi, mid, low], axis=0)


def joined(value):
    k = value.shape[0] // 3
    return value[:k] + (value[k : 2 * k] + value[2 * k :])


def halo_kernel(G, M, f_ref, a_ref, fe, ae, sx, rx, sy, ry, sc, rc):
    K, X, Y, Z = f_ref.shape
    bx, by = X // CELL, Y // CELL
    g, m = lax.axis_index("grp"), lax.axis_index("mem")
    flat = f_ref.reshape(K * X * Y, Z)

    sides = []
    if G > 1:
        sides += [(g > 0, {"grp": g - 1}), (g < G - 1, {"grp": g + 1})]
    if M > 1:
        sides += [(m > 0, {"mem": m - 1}), (m < M - 1, {"mem": m + 1})]
    barrier = pltpu.get_barrier_semaphore()
    for there, dev in sides:

        @pl.when(there)
        def _(dev=dev):
            pl.semaphore_signal(barrier, inc=1, device_id=dev, device_id_type=MESH)

    @pl.loop(0, X)
    def _(x):
        for y in range(Y):
            fe[HALO + x, HALO + y] = flat[pl.ds(x * Y + y, K, stride=X * Y), :]

    ae[1 : 1 + bx, 1 : 1 + by] = a_ref[...]

    def blank(start):
        @pl.loop(start, start + HALO)
        def _(x):
            fe[x, HALO : HALO + Y] = jnp.zeros((Y,) + fe.shape[2:], F32)

    @pl.when(g == 0)
    def _():
        blank(0)
        ae[0:1, 1 : 1 + by] = jnp.zeros((1, by) + ae.shape[2:], jnp.int32)

    @pl.when(g == G - 1)
    def _():
        blank(HALO + X)
        ae[1 + bx :, 1 : 1 + by] = jnp.zeros((1, by) + ae.shape[2:], jnp.int32)

    @pl.when(m == 0)
    def _():
        @pl.loop(0, X + 2 * HALO)
        def _(x):
            fe[x, 0:HALO] = jnp.zeros((HALO,) + fe.shape[2:], F32)

        ae[:, 0:1] = jnp.zeros((bx + 2, 1) + ae.shape[2:], jnp.int32)

    @pl.when(m == M - 1)
    def _():
        @pl.loop(0, X + 2 * HALO)
        def _(x):
            fe[x, HALO + Y :] = jnp.zeros((HALO,) + fe.shape[2:], F32)

        ae[:, 1 + by :] = jnp.zeros((bx + 2, 1) + ae.shape[2:], jnp.int32)

    def beside(index, count):
        return (index + count - 1) // count + (2 * (count - 1) - index) // count

    pl.semaphore_wait(barrier, beside(g, G) + beside(m, M))

    def copy(ref, src, dst, dev, sems, slot):
        return pltpu.make_async_remote_copy(
            src_ref=ref.at[src],
            dst_ref=ref.at[dst],
            send_sem=sems[0].at[slot],
            recv_sem=sems[1].at[slot],
            device_id=dev,
            device_id_type=MESH,
        )

    def faces(down, axis, dev):
        out = []
        n, other = ((X, Y), (Y, X))[axis]
        nb, otherb = ((bx, by), (by, bx))[axis]
        for slot, (ref, h, length, across) in enumerate(
            ((fe, HALO, n, other), (ae, 1, nb, otherb))
        ):
            src = pl.ds(h if down else length, h)
            dst = pl.ds(length + h if down else 0, h)
            whole = pl.ds(h, across)
            pick = (lambda d: (d, whole)) if axis == 0 else (lambda d: (whole, d))
            base = (0 if down else 2) + slot
            out.append(copy(ref, pick(src), pick(dst), dev, (sx, rx) if axis == 0 else (sy, ry), base))
        return out

    def corners(down, dev):
        out = []
        slot = 0 if down else 2 * HALO
        for d in range(1, HALO):
            width = HALO - d
            src = pl.ds(HALO if down else HALO + Y - width, width)
            dst = pl.ds(HALO + Y if down else HALO - width, width)
            for row in (HALO - d, HALO + X - 1 + d):
                out.append(copy(fe, (row, src), (row, dst), dev, (sc, rc), slot))
                slot += 1
        src = pl.ds(1 if down else by, 1)
        dst = pl.ds(1 + by if down else 0, 1)
        for row in (0, bx + 1):
            out.append(copy(ae, (row, src), (row, dst), dev, (sc, rc), slot))
            slot += 1
        return out

    def each(index, count, name, body):
        if count > 1:
            pl.when(index > 0)(lambda: body(True, {name: index - 1}))
            pl.when(index < count - 1)(lambda: body(False, {name: index + 1}))

    def start_faces(axis):
        def body(down, dev):
            for c in faces(down, axis, dev):
                c.start()

        return body

    def end_faces(axis):
        def body(down, dev):
            for c in faces(down, axis, dev):
                c.wait_send()
            for c in faces(not down, axis, dev):
                c.wait_recv()

        return body

    def start_corners(down, dev):
        for c in corners(down, dev):
            c.start()

    def end_corners(down, dev):
        for c in corners(down, dev):
            c.wait_send()
        for c in corners(not down, dev):
            c.wait_recv()

    each(g, G, "grp", start_faces(0))
    each(m, M, "mem", start_faces(1))
    each(g, G, "grp", end_faces(0))
    each(m, M, "mem", start_corners)
    each(m, M, "mem", end_faces(1))
    each(m, M, "mem", end_corners)


def sweep(src, x0, x1, y0, y1, emit):
    Z = src.shape[-1]
    lane = lax.broadcasted_iota(jnp.int32, (src.shape[2], Z), 1)
    first, last = lane == 0, lane == Z - 1

    @pl.loop(x0, x1)
    def _(x):
        prev, here = src[x, y0 - 1], src[x, y0]
        for y in range(y0, y1):
            after = src[x, y + 1]
            near = src[x - 1, y] + src[x + 1, y] + (prev + after)
            low = jnp.where(first, 0.0, pltpu.roll(here, 1, 1))
            high = jnp.where(last, 0.0, pltpu.roll(here, Z - 1, 1))
            emit(x, y, here, near + (low + high))
            prev, here = here, after


def clear_outside(ref, G, M, X, Y, width):
    g, m = lax.axis_index("grp"), lax.axis_index("mem")
    h = HALO
    rest = ref.shape[2:]

    def rows(start):
        @pl.loop(start, start + width)
        def _(x):
            ref[x] = jnp.zeros(ref.shape[1:], F32)

    def columns(start):
        @pl.loop(h - width, h + X + width)
        def _(x):
            ref[x, start : start + width] = jnp.zeros((width,) + rest, F32)

    pl.when(g == 0)(lambda: rows(h - width))
    pl.when(g == G - 1)(lambda: rows(h + X))
    pl.when(m == 0)(lambda: columns(h - width))
    pl.when(m == M - 1)(lambda: columns(h + Y))


def pre_kernel(G, M, chunk, side, fe, ids_ref, s3, d_ref, s2, means):
    Xe, Ye, K, Z = fe.shape
    X, Y = Xe - 2 * HALO, Ye - 2 * HALO
    bx, by, bz = X // CELL, Y // CELL, Z // CELL
    w = WEIGHT

    def second(x, y, c, near):
        s2[x, y] = w * ((2.0 - 6.0 * w) * c + w * near)

    sweep(fe, 1, Xe - 1, 1, Ye - 1, second)
    clear_outside(s2, G, M, X, Y, 3)

    def third(x, y, c, near):
        s3[x, y] = (1.0 - 6.0 * w) * c + w * (fe[x, y] + near)

    sweep(s2, 2, Xe - 2, 2, Ye - 2, third)
    clear_outside(s3, G, M, X, Y, 2)

    def residual(x, y, c, near):
        s2[x, y] = fe[x, y] - 6.0 * c + near

    sweep(s3, HALO, HALO + X, HALO, HALO + Y, residual)

    rows = lax.broadcasted_iota(jnp.int32, (by * Z, by * bz), 0)
    cols = lax.broadcasted_iota(jnp.int32, (by * Z, by * bz), 1)
    spread = jnp.where(rows // CELL == cols, 1.0 / CELL**3, 0.0).astype(BF16)
    for i in range(bx):
        parts = []
        for j in range(by):
            total = None
            for p in range(CELL):
                for q in range(CELL):
                    v = s2[HALO + i * CELL + p, HALO + j * CELL + q]
                    total = v if total is None else total + v
            parts.append(total)
        line = jnp.concatenate(parts, axis=1)
        means[:, i * by * bz : (i + 1) * by * bz] = joined(
            jnp.dot(pieces(line), spread, preferred_element_type=F32)
        )
    split = pieces(means[...])
    ids = ids_ref[...]
    count = bx * by * bz

    entry = lax.broadcasted_iota(jnp.int32, (chunk, count), 0)

    @pl.loop(0, d_ref.shape[1])
    def _(h):
        for c in range(2):
            owner = (h // side) * 2 * side + 2 * (h % side) + c
            hot = jnp.where(entry == ids - owner * chunk, 1.0, 0.0).astype(BF16)
            got = lax.dot_general(
                split, hot, (((1,), (1,)), ((), ())), preferred_element_type=F32
            )
            d_ref[c, h] = joined(got)


def coarse_kernel(
    G, M, n_own, d_ref, fac_ref, x_ref, r, pair, e, psend, precv, ssend, srecv, gsend, grecv, fsend, frecv
):
    n = G * M // 2
    side = n_own // 2
    held = side * M
    g, m = lax.axis_index("grp"), lax.axis_index("mem")
    core = lax.rem(g, 2)
    me = (g // 2) * M + m
    own = m * side + g // 2
    q, bs = fac_ref.shape[0], fac_ref.shape[1]
    everyone = n_own == G
    partner = {"grp": g + 1 - 2 * core, "mem": m}

    def device(i):
        return {"grp": 2 * (i // M) + core, "mem": i % M}

    def peer(t):
        return lax.rem(me + t, n)

    def send(src, dst, ssem, rsem, to):
        return pltpu.make_async_remote_copy(
            src_ref=src, dst_ref=dst, send_sem=ssem, recv_sem=rsem, device_id=to, device_id_type=MESH
        )

    barrier = pltpu.get_barrier_semaphore()
    pl.semaphore_signal(barrier, inc=1, device_id=partner, device_id_type=MESH)

    @pl.loop(1, n)
    def _(t):
        pl.semaphore_signal(barrier, inc=1, device_id=device(peer(t)), device_id_type=MESH)

    pl.semaphore_wait(barrier, n)

    def owning(i, body):
        if everyone:
            body()
        else:
            pl.when(i // M < side)(body)

    swap = send(d_ref.at[1 - core], pair, psend, precv, partner)
    swap.start()
    swap.wait()

    @pl.loop(0, held)
    def _(h):
        e[h] = d_ref[core, h] + pair[h]

    @pl.loop(1, n)
    def _(t):
        to = peer(t)
        block = (to % M) * side + to // M
        owning(to, lambda: send(e.at[block], r.at[me], ssend, srecv, device(to)).start())

    def wait_bytes(ref, count, sem):
        if count > 0:
            part = ref.at[pl.ds(0, count)]
            pltpu.make_async_copy(part, part, sem).wait()

    def solve():
        wait_bytes(r, n - 1, srecv)

        def add(t, total):
            return total + r[peer(t)]

        total = lax.fori_loop(1, n, add, e[own])
        for b in range(q):
            rhs = total[:, b * bs : (b + 1) * bs]
            inner = lax.dot_general(
                rhs,
                fac_ref[b],
                (((1,), (1,)), ((), ())),
                precision=lax.Precision.HIGHEST,
                preferred_element_type=F32,
            )
            x_ref[core, own, :, b * bs : (b + 1) * bs] = lax.dot_general(
                inner,
                fac_ref[b],
                (((1,), (0,)), ((), ())),
                precision=lax.Precision.HIGHEST,
                preferred_element_type=F32,
            )

        @pl.loop(1, n)
        def _(t):
            mine = x_ref.at[core, own]
            send(mine, mine, gsend, grecv, device(peer(t))).start()

    owning(me, solve)

    if everyone:
        wait_bytes(e, held - 1, ssend)
        wait_bytes(e, held - 1, grecv)
        wait_bytes(r, n - 1, gsend)
    else:
        mine = g < n_own

        @pl.when(mine)
        def _():
            wait_bytes(e, held - 1, ssend)
            wait_bytes(e, held - 1, grecv)
            wait_bytes(r, n - 1, gsend)

        @pl.when(jnp.logical_not(mine))
        def _():
            wait_bytes(e, held, ssend)
            wait_bytes(e, held, grecv)

    forward = send(x_ref.at[core], x_ref.at[core], fsend, frecv, partner)
    forward.start()
    forward.wait()


def post_kernel(G, M, bs, side, fe, s3, ae, x_ref, o_ref, lifted, sol):
    Xe, Ye, K, Z = fe.shape
    X, Y = Xe - 2 * HALO, Ye - 2 * HALO
    bx, by, bz = X // CELL + 2, Y // CELL + 2, Z // CELL
    w = WEIGHT
    half = 8
    q = x_ref.shape[3] // bs
    per = Z // bz
    groups = [range(s, min(s + per, by)) for s in range(0, by, per)]
    lane = lax.broadcasted_iota(jnp.int32, (half, Z), 1)

    def pick(table, index):
        return jnp.take_along_axis(table, index, axis=1)

    def lines(base, count):
        rows = [(base + d, group) for d in range(count) for group in groups]
        inner, outer = [], []
        for i, group in rows:
            index = None
            for slot, j in enumerate(group):
                packed = pick(ae[i, j], (lane % bz) * CELL)
                index = packed if index is None else jnp.where(lane // bz == slot, packed, index)
            inner.append(index % bs)
            outer.append(index // bs)
        halves = K // half

        def body(h, found):
            out = list(found)
            for c in range(2):
                owner = (h // side) * 2 * side + 2 * (h % side) + c
                for b in range(q):
                    tables = [
                        x_ref[c, h, t * half : (t + 1) * half, b * bs : (b + 1) * bs]
                        for t in range(halves)
                    ]
                    for e in range(len(rows)):
                        hit = outer[e] == owner * q + b
                        for t in range(halves):
                            k = e * halves + t
                            out[k] = jnp.where(hit, pick(tables[t], inner[e]), out[k])
            return tuple(out)

        zeros = tuple(jnp.zeros((half, Z), F32) for _ in range(len(rows) * halves))
        found = lax.fori_loop(0, x_ref.shape[1], body, zeros)
        for e, (i, group) in enumerate(rows):
            for slot, j in enumerate(group):
                wide = [
                    pick(found[e * halves + t], lane // CELL + slot * bz) for t in range(halves)
                ]
                value = jnp.concatenate(wide, axis=0)
                for p in range(CELL):
                    for r in range(CELL):
                        lifted[i * CELL + p, j * CELL + r] = value

    batch = max(d for d in (1, 2, 3) if bx % d == 0)

    @pl.loop(0, bx // batch)
    def _(i):
        lines(i * batch, batch)

    clear_outside(lifted, G, M, X, Y, HALO)

    def start(x, y, c, near):
        sol[x, y] = s3[x, y] + ((1.0 - 6.0 * w) * c + w * near)

    sweep(lifted, 2, Xe - 2, 2, Ye - 2, start)
    clear_outside(sol, G, M, X, Y, 2)

    def first(x, y, c, near):
        lifted[x, y] = (1.0 - 6.0 * w) * c + w * (fe[x, y] + near)

    sweep(sol, 3, Xe - 3, 3, Ye - 3, first)
    clear_outside(lifted, G, M, X, Y, 1)

    flat = o_ref.reshape(K * X * Y, Z)

    def last(x, y, c, near):
        flat[pl.ds((x - HALO) * Y + (y - HALO), K, stride=X * Y), :] = (
            1.0 - 6.0 * w
        ) * c + w * (fe[x, y] + near)

    sweep(lifted, HALO, HALO + X, HALO, HALO + Y, last)


def shards(G, M, forcing, aggregate, factors):
    K, X, Y, Z = forcing.shape
    bx, by, bz = aggregate.shape
    Xe, Ye = X + 2 * HALO, Y + 2 * HALO
    local_blocks, bs = factors.shape[0], factors.shape[1]
    q = -(-local_blocks // G)
    n_own = local_blocks // q
    chunk = q * bs
    owners = n_own * M
    sd = jax.ShapeDtypeStruct

    wide_ids = jnp.broadcast_to(
        jnp.repeat(aggregate, CELL, axis=2)[:, :, None, :], (bx, by, 8, Z)
    )
    fe, ae = pl.pallas_call(
        functools.partial(halo_kernel, G, M),
        out_shape=(sd((Xe, Ye, K, Z), F32), sd((bx + 2, by + 2, 8, Z), jnp.int32)),
        in_specs=[vmem_spec()] * 2,
        out_specs=(vmem_spec(),) * 2,
        scratch_shapes=[pltpu.SemaphoreType.DMA((4,))] * 4
        + [pltpu.SemaphoreType.DMA((4 * HALO,))] * 2,
        compiler_params=params(collective_id=0, has_side_effects=True),
        name="halo",
    )(forcing, wide_ids)

    s3, dense = pl.pallas_call(
        functools.partial(pre_kernel, G, M, chunk, n_own // 2),
        out_shape=(sd((Xe, Ye, K, Z), F32), sd((2, owners // 2, K, chunk), F32)),
        in_specs=[vmem_spec()] * 2,
        out_specs=(vmem_spec(),) * 2,
        scratch_shapes=[VMEM((Xe, Ye, K, Z), F32), VMEM((K, bx * by * bz), F32)],
        compiler_params=params(),
        name="pre",
    )(fe, aggregate.reshape(1, -1))

    g = lax.axis_index("grp")
    mine = lax.dynamic_slice_in_dim(factors, jnp.minimum(g, n_own - 1) * q, q, axis=0)
    fix = pl.pallas_call(
        functools.partial(coarse_kernel, G, M, n_own),
        out_shape=sd((2, owners // 2, K, chunk), F32),
        in_specs=[vmem_spec()] * 2,
        out_specs=vmem_spec(),
        scratch_shapes=[VMEM((G * M // 2, K, chunk), F32)] + [VMEM((owners // 2, K, chunk), F32)] * 2 + [pltpu.SemaphoreType.DMA] * 8,
        compiler_params=params(collective_id=1, has_side_effects=True),
        name="coarse",
    )(dense, mine)

    return pl.pallas_call(
        functools.partial(post_kernel, G, M, bs, n_own // 2),
        out_shape=sd((K, X, Y, Z), F32),
        in_specs=[vmem_spec()] * 4,
        out_specs=vmem_spec(),
        scratch_shapes=[VMEM((Xe, Ye, K, Z), F32)] * 2,
        compiler_params=params(),
        name="post",
    )(fe, s3, ae, fix)


def solution(mesh):
    placed = (P(None, "grp", "mem", None), P("grp", "mem", None), P("mem", None, None))
    body = functools.partial(shards, mesh.shape["grp"], mesh.shape["mem"])
    return jax.shard_map(
        body, mesh=mesh, in_specs=placed, out_specs=P(None, "grp", "mem", None), check_vma=False
    )
```

```python
import functools

import jax
import jax.numpy as jnp
from jax import lax
from jax.experimental import pallas as pl
from jax.experimental.pallas import tpu as pltpu
from jax.sharding import PartitionSpec as P

NC = 8192
relaxation = 0.8
WEIGHT = relaxation / 6.0
CELL = 4
HALO = 4
F32 = jnp.float32
BF16 = jnp.bfloat16
MESH = pl.DeviceIdType.MESH
VMEM = pltpu.VMEM


def vmem_spec():
    return pl.BlockSpec(memory_space=pltpu.VMEM)


def any_spec():
    return pl.BlockSpec(memory_space=pl.ANY)


def params(**kw):
    return pltpu.CompilerParams(vmem_limit_bytes=60 * 1024 * 1024, **kw)


def pieces(value):
    hi = value.astype(BF16)
    rest = value - hi.astype(F32)
    mid = rest.astype(BF16)
    low = (rest - mid.astype(F32)).astype(BF16)
    return jnp.concatenate([hi, mid, low], axis=0)


def joined(value):
    k = value.shape[0] // 3
    return value[:k] + (value[k : 2 * k] + value[2 * k :])


def sweep(src, x0, x1, y0, y1, emit):
    Z = src.shape[-1]
    lane = lax.broadcasted_iota(jnp.int32, (src.shape[2], Z), 1)
    first, last = lane == 0, lane == Z - 1

    @pl.loop(x0, x1)
    def _(x):
        prev, here = src[x, y0 - 1], src[x, y0]
        for y in range(y0, y1):
            after = src[x, y + 1]
            near = src[x - 1, y] + src[x + 1, y] + (prev + after)
            low = jnp.where(first, 0.0, pltpu.roll(here, 1, 1))
            high = jnp.where(last, 0.0, pltpu.roll(here, Z - 1, 1))
            emit(x, y, here, near + (low + high))
            prev, here = here, after


def clear_outside(ref, G, M, X, Y, width):
    g, m = lax.axis_index("grp"), lax.axis_index("mem")
    h = HALO
    rest = ref.shape[2:]

    def rows(start):
        @pl.loop(start, start + width)
        def _(x):
            ref[x] = jnp.zeros(ref.shape[1:], F32)

    def columns(start):
        @pl.loop(h - width, h + X + width)
        def _(x):
            ref[x, start : start + width] = jnp.zeros((width,) + rest, F32)

    pl.when(g == 0)(lambda: rows(h - width))
    pl.when(g == G - 1)(lambda: rows(h + X))
    pl.when(m == 0)(lambda: columns(h - width))
    pl.when(m == M - 1)(lambda: columns(h + Y))


def down_kernel(
    G, M, n_own, f_ref, a_ref, fac_hbm, fe_out, s3_out, ae, x_ref,
    fe, s3, s2, means, hot, d_ref, r, pair, e, fac_ref,
    sx, rx, sy, ry, sc, rc, local, psend, precv, ssend, srecv, gsend, grecv, fsend, frecv,
):
    K, X, Y, Z = f_ref.shape
    Xe, Ye = X + 2 * HALO, Y + 2 * HALO
    bx, by, bz = a_ref.shape
    w = WEIGHT
    n = G * M // 2
    side = n_own // 2
    held = side * M
    g, m = lax.axis_index("grp"), lax.axis_index("mem")
    core = lax.rem(g, 2)
    me = (g // 2) * M + m
    own = m * side + g // 2
    q, bs = fac_ref.shape[0], fac_ref.shape[1]
    chunk = q * bs
    everyone = n_own == G
    partner = {"grp": g + 1 - 2 * core, "mem": m}
    flat = f_ref.reshape(K * X * Y, Z)

    def device(i):
        return {"grp": 2 * (i // M) + core, "mem": i % M}

    def peer(t):
        return lax.rem(me + t, n)

    def send(src, dst, ssem, rsem, to):
        return pltpu.make_async_remote_copy(
            src_ref=src, dst_ref=dst, send_sem=ssem, recv_sem=rsem, device_id=to, device_id_type=MESH
        )

    barrier = pltpu.get_barrier_semaphore()

    def greet(to):
        pl.semaphore_signal(barrier, inc=1, device_id=to, device_id_type=MESH)

    greet(partner)
    pl.when(jnp.logical_and(core == 0, g > 0))(lambda: greet({"grp": g - 1, "mem": m}))
    pl.when(jnp.logical_and(core == 1, g < G - 1))(lambda: greet({"grp": g + 1, "mem": m}))

    @pl.loop(1, n)
    def _(t):
        greet(device(peer(t)))

    first = lax.rem(g, n_own) * q
    fetch = pltpu.make_async_copy(fac_hbm.at[pl.ds(first, q)], fac_ref, local.at[0])
    fetch.start()

    @pl.loop(0, X)
    def _(x):
        for y in range(Y):
            fe[HALO + x, HALO + y] = flat[pl.ds(x * Y + y, K, stride=X * Y), :]

    for i in range(bx):
        for j in range(by):
            row = a_ref[i, j : j + 1, :]
            wide = jnp.concatenate([row] * (Z // bz), axis=1)
            ae[1 + i, 1 + j] = jnp.broadcast_to(wide, ae.shape[2:])

    def blank(start):
        @pl.loop(start, start + HALO)
        def _(x):
            fe[x, HALO : HALO + Y] = jnp.zeros((Y,) + fe.shape[2:], F32)

    def blank_side(start):
        @pl.loop(0, Xe)
        def _(x):
            fe[x, start : start + HALO] = jnp.zeros((HALO,) + fe.shape[2:], F32)

    @pl.when(g == 0)
    def _():
        blank(0)
        ae[0:1, 1 : 1 + by] = jnp.zeros((1, by) + ae.shape[2:], jnp.int32)

    @pl.when(g == G - 1)
    def _():
        blank(HALO + X)
        ae[1 + bx :, 1 : 1 + by] = jnp.zeros((1, by) + ae.shape[2:], jnp.int32)

    @pl.when(m == 0)
    def _():
        blank_side(0)
        ae[:, 0:1] = jnp.zeros((bx + 2, 1) + ae.shape[2:], jnp.int32)

    @pl.when(m == M - 1)
    def _():
        blank_side(HALO + Y)
        ae[:, 1 + by :] = jnp.zeros((bx + 2, 1) + ae.shape[2:], jnp.int32)

    pl.semaphore_wait(barrier, n + (g + G - 1) // G + (2 * (G - 1) - g) // G - 1)

    def copy(ref, src, dst, dev, sems, slot):
        return pltpu.make_async_remote_copy(
            src_ref=ref.at[src],
            dst_ref=ref.at[dst],
            send_sem=sems[0].at[slot],
            recv_sem=sems[1].at[slot],
            device_id=dev,
            device_id_type=MESH,
        )

    def faces(down, axis, dev):
        out = []
        n, other = ((X, Y), (Y, X))[axis]
        nb, otherb = ((bx, by), (by, bx))[axis]
        for slot, (ref, h, length, across) in enumerate(
            ((fe, HALO, n, other), (ae, 1, nb, otherb))
        ):
            src = pl.ds(h if down else length, h)
            dst = pl.ds(length + h if down else 0, h)
            whole = pl.ds(h, across)
            pick = (lambda d: (d, whole)) if axis == 0 else (lambda d: (whole, d))
            base = (0 if down else 2) + slot
            out.append(copy(ref, pick(src), pick(dst), dev, (sx, rx) if axis == 0 else (sy, ry), base))
        return out

    def corners(down, dev):
        out = []
        slot = 0 if down else 2 * HALO
        for d in range(1, HALO):
            width = HALO - d
            src = pl.ds(HALO if down else HALO + Y - width, width)
            dst = pl.ds(HALO + Y if down else HALO - width, width)
            for row in (HALO - d, HALO + X - 1 + d):
                out.append(copy(fe, (row, src), (row, dst), dev, (sc, rc), slot))
                slot += 1
        src = pl.ds(1 if down else by, 1)
        dst = pl.ds(1 + by if down else 0, 1)
        for row in (0, bx + 1):
            out.append(copy(ae, (row, src), (row, dst), dev, (sc, rc), slot))
            slot += 1
        return out

    def each(index, count, name, body):
        if count > 1:
            pl.when(index > 0)(lambda: body(True, {name: index - 1}))
            pl.when(index < count - 1)(lambda: body(False, {name: index + 1}))

    def start_faces(axis):
        def body(down, dev):
            for c in faces(down, axis, dev):
                c.start()

        return body

    def end_faces(axis):
        def body(down, dev):
            for c in faces(down, axis, dev):
                c.wait_send()
            for c in faces(not down, axis, dev):
                c.wait_recv()

        return body

    def start_corners(down, dev):
        for c in corners(down, dev):
            c.start()

    def end_corners(down, dev):
        for c in corners(down, dev):
            c.wait_send()
        for c in corners(not down, dev):
            c.wait_recv()

    each(g, G, "grp", start_faces(0))
    each(m, M, "mem", start_faces(1))


    def second(x, y, c, near):
        s2[x, y] = w * ((2.0 - 6.0 * w) * c + w * near)

    def third(x, y, c, near):
        s3[x, y] = (1.0 - 6.0 * w) * c + w * (fe[x, y] + near)

    def residual(x, y, c, near):
        s2[x, y] = fe[x, y] - 6.0 * c + near

    def inner(src, depth, emit):
        lo = HALO + depth
        sweep(src, lo, HALO + X - depth, lo, HALO + Y - depth, emit)

    def ring(src, depth, reach, emit):
        lo, hx, hy = HALO + depth, HALO + X - depth, HALO + Y - depth
        y0, y1 = HALO - reach, HALO + Y + reach
        sweep(src, HALO - reach, lo, y0, y1, emit)
        sweep(src, hx, HALO + X + reach, y0, y1, emit)
        sweep(src, lo, hx, y0, lo, emit)
        sweep(src, lo, hx, hy, y1, emit)

    inner(fe, 1, second)
    inner(s2, 2, third)

    count = bx * by * bz
    ids = jnp.concatenate(
        [a_ref[i, j : j + 1, :] for i in range(bx) for j in range(by)], axis=1
    )
    entry = lax.broadcasted_iota(jnp.int32, (chunk, count), 0)

    def owner_of(c, h):
        return (h // side) * 2 * side + 2 * (h % side) + c

    @pl.loop(0, held)
    def _(h):
        for c in range(2):
            hit = entry == ids - owner_of(c, h) * chunk
            hot[c, h] = jnp.where(hit, 1.0, 0.0).astype(BF16)

    each(g, G, "grp", end_faces(0))
    each(m, M, "mem", start_corners)
    each(m, M, "mem", end_faces(1))
    each(m, M, "mem", end_corners)

    fe_copy = pltpu.make_async_copy(fe, fe_out, local.at[1])
    fe_copy.start()

    ring(fe, 1, 3, second)
    clear_outside(s2, G, M, X, Y, 3)
    ring(s2, 2, 2, third)
    clear_outside(s3, G, M, X, Y, 2)
    s3_copy = pltpu.make_async_copy(s3, s3_out, local.at[2])
    s3_copy.start()
    inner(s3, 0, residual)

    rows = lax.broadcasted_iota(jnp.int32, (by * Z, by * bz), 0)
    cols = lax.broadcasted_iota(jnp.int32, (by * Z, by * bz), 1)
    spread = jnp.where(rows // CELL == cols, 1.0 / CELL**3, 0.0).astype(BF16)
    for i in range(bx):
        parts = []
        for j in range(by):
            total = None
            for p in range(CELL):
                for t in range(CELL):
                    v = s2[HALO + i * CELL + p, HALO + j * CELL + t]
                    total = v if total is None else total + v
            parts.append(total)
        line = jnp.concatenate(parts, axis=1)
        means[:, i * by * bz : (i + 1) * by * bz] = joined(
            jnp.dot(pieces(line), spread, preferred_element_type=F32)
        )
    split = pieces(means[...])

    def scatter(c):
        @pl.loop(0, held)
        def _(h):
            got = lax.dot_general(
                split, hot[c, h], (((1,), (1,)), ((), ())), preferred_element_type=F32
            )
            d_ref[c, h] = joined(got)

    scatter(1 - core)
    def owning(i, body):
        if everyone:
            body()
        else:
            pl.when(i // M < side)(body)

    swap = send(d_ref.at[1 - core], pair, psend, precv, partner)
    swap.start()
    scatter(core)
    swap.wait()

    @pl.loop(0, held)
    def _(h):
        e[h] = d_ref[core, h] + pair[h]

    @pl.loop(1, n)
    def _(t):
        to = peer(t)
        block = (to % M) * side + to // M
        owning(to, lambda: send(e.at[block], r.at[me], ssend, srecv, device(to)).start())

    def wait_bytes(ref, count, sem):
        if count > 0:
            part = ref.at[pl.ds(0, count)]
            pltpu.make_async_copy(part, part, sem).wait()

    fetch.wait()

    def solve():
        wait_bytes(r, n - 1, srecv)

        def add(t, total):
            return total + r[peer(t)]

        total = lax.fori_loop(1, n, add, e[own])
        for b in range(q):
            rhs = total[:, b * bs : (b + 1) * bs]
            inner = lax.dot_general(
                rhs,
                fac_ref[b],
                (((1,), (1,)), ((), ())),
                precision=lax.Precision.HIGHEST,
                preferred_element_type=F32,
            )
            x_ref[core, own, :, b * bs : (b + 1) * bs] = lax.dot_general(
                inner,
                fac_ref[b],
                (((1,), (0,)), ((), ())),
                precision=lax.Precision.HIGHEST,
                preferred_element_type=F32,
            )

        @pl.loop(1, n)
        def _(t):
            mine = x_ref.at[core, own]
            send(mine, mine, gsend, grecv, device(peer(t))).start()

    owning(me, solve)

    if everyone:
        wait_bytes(e, held - 1, ssend)
        wait_bytes(e, held - 1, grecv)
        wait_bytes(r, n - 1, gsend)
    else:
        mine = g < n_own

        @pl.when(mine)
        def _():
            wait_bytes(e, held - 1, ssend)
            wait_bytes(e, held - 1, grecv)
            wait_bytes(r, n - 1, gsend)

        @pl.when(jnp.logical_not(mine))
        def _():
            wait_bytes(e, held, ssend)
            wait_bytes(e, held, grecv)

    forward = send(x_ref.at[core], x_ref.at[core], fsend, frecv, partner)
    forward.start()
    forward.wait()
    fe_copy.wait()
    s3_copy.wait()


def post_kernel(G, M, bs, side, fe_hbm, s3_hbm, ae, x_ref, o_ref, lifted, sol, fe, s3, sems):
    loads = [
        pltpu.make_async_copy(s3_hbm, s3, sems.at[0]),
        pltpu.make_async_copy(fe_hbm, fe, sems.at[1]),
    ]
    for c in loads:
        c.start()
    Xe, Ye, K, Z = fe.shape
    X, Y = Xe - 2 * HALO, Ye - 2 * HALO
    bx, by, bz = X // CELL + 2, Y // CELL + 2, Z // CELL
    w = WEIGHT
    half = 8
    q = x_ref.shape[3] // bs
    per = Z // bz
    groups = [range(s, min(s + per, by)) for s in range(0, by, per)]
    lane = lax.broadcasted_iota(jnp.int32, (half, Z), 1)

    def pick(table, index):
        return jnp.take_along_axis(table, index, axis=1)

    def lines(base, count):
        rows = [(base + d, group) for d in range(count) for group in groups]
        inner, outer = [], []
        for i, group in rows:
            index = None
            for slot, j in enumerate(group):
                packed = ae[i, j]
                index = packed if index is None else jnp.where(lane // bz == slot, packed, index)
            inner.append(index % bs)
            outer.append(index // bs)
        halves = K // half

        def body(h, found):
            out = list(found)
            for c in range(2):
                owner = (h // side) * 2 * side + 2 * (h % side) + c
                for b in range(q):
                    tables = [
                        x_ref[c, h, t * half : (t + 1) * half, b * bs : (b + 1) * bs]
                        for t in range(halves)
                    ]
                    for e in range(len(rows)):
                        hit = outer[e] == owner * q + b
                        for t in range(halves):
                            k = e * halves + t
                            out[k] = jnp.where(hit, pick(tables[t], inner[e]), out[k])
            return tuple(out)

        zeros = tuple(jnp.zeros((half, Z), F32) for _ in range(len(rows) * halves))
        found = lax.fori_loop(0, x_ref.shape[1], body, zeros)
        for e, (i, group) in enumerate(rows):
            for slot, j in enumerate(group):
                wide = [
                    pick(found[e * halves + t], lane // CELL + slot * bz) for t in range(halves)
                ]
                value = jnp.concatenate(wide, axis=0)
                for p in range(CELL):
                    for r in range(CELL):
                        lifted[i * CELL + p, j * CELL + r] = value

    batch = max(d for d in (1, 2, 3) if bx % d == 0)

    @pl.loop(0, bx // batch)
    def _(i):
        lines(i * batch, batch)

    clear_outside(lifted, G, M, X, Y, HALO)
    loads[0].wait()

    def start(x, y, c, near):
        sol[x, y] = s3[x, y] + ((1.0 - 6.0 * w) * c + w * near)

    sweep(lifted, 2, Xe - 2, 2, Ye - 2, start)
    clear_outside(sol, G, M, X, Y, 2)
    loads[1].wait()

    def first(x, y, c, near):
        lifted[x, y] = (1.0 - 6.0 * w) * c + w * (fe[x, y] + near)

    sweep(sol, 3, Xe - 3, 3, Ye - 3, first)
    clear_outside(lifted, G, M, X, Y, 1)

    flat = o_ref.reshape(K * X * Y, Z)

    def last(x, y, c, near):
        flat[pl.ds((x - HALO) * Y + (y - HALO), K, stride=X * Y), :] = (
            1.0 - 6.0 * w
        ) * c + w * (fe[x, y] + near)

    sweep(lifted, HALO, HALO + X, HALO, HALO + Y, last)


def shards(G, M, forcing, aggregate, factors):
    K, X, Y, Z = forcing.shape
    bx, by, bz = aggregate.shape
    Xe, Ye = X + 2 * HALO, Y + 2 * HALO
    local_blocks, bs = factors.shape[0], factors.shape[1]
    q = -(-local_blocks // G)
    n_own = local_blocks // q
    chunk = q * bs
    owners = n_own * M
    sd = jax.ShapeDtypeStruct

    fe, s3, ae, fix = pl.pallas_call(
        functools.partial(down_kernel, G, M, n_own),
        out_shape=(
            sd((Xe, Ye, K, Z), F32),
            sd((Xe, Ye, K, Z), F32),
            sd((bx + 2, by + 2, 8, Z), jnp.int32),
            sd((2, owners // 2, K, chunk), F32),
        ),
        in_specs=[vmem_spec(), vmem_spec(), any_spec()],
        out_specs=(any_spec(), any_spec(), vmem_spec(), vmem_spec()),
        scratch_shapes=[VMEM((Xe, Ye, K, Z), F32)] * 3
        + [
            VMEM((K, bx * by * bz), F32),
            VMEM((2, owners // 2, chunk, bx * by * bz), BF16),
            VMEM((2, owners // 2, K, chunk), F32),
            VMEM((G * M // 2, K, chunk), F32),
            VMEM((owners // 2, K, chunk), F32),
            VMEM((owners // 2, K, chunk), F32),
            VMEM((q, bs, bs), F32),
        ]
        + [pltpu.SemaphoreType.DMA((4,))] * 4
        + [pltpu.SemaphoreType.DMA((4 * HALO,))] * 2
        + [pltpu.SemaphoreType.DMA((3,))]
        + [pltpu.SemaphoreType.DMA] * 8,
        compiler_params=params(collective_id=0, has_side_effects=True),
        name="down",
    )(forcing, aggregate, factors)

    return pl.pallas_call(
        functools.partial(post_kernel, G, M, bs, n_own // 2),
        out_shape=sd((K, X, Y, Z), F32),
        in_specs=[any_spec(), any_spec(), vmem_spec(), vmem_spec()],
        out_specs=vmem_spec(),
        scratch_shapes=[VMEM((Xe, Ye, K, Z), F32)] * 4 + [pltpu.SemaphoreType.DMA((2,))],
        compiler_params=params(),
        name="post",
    )(fe, s3, ae, fix)


def solution(mesh):
    placed = (P(None, "grp", "mem", None), P("grp", "mem", None), P("mem", None, None))
    body = functools.partial(shards, mesh.shape["grp"], mesh.shape["mem"])
    return jax.shard_map(
        body, mesh=mesh, in_specs=placed, out_specs=P(None, "grp", "mem", None), check_vma=False
    )
```

```python
import functools

import jax
import jax.numpy as jnp
from jax import lax
from jax.experimental import pallas as pl
from jax.experimental.pallas import tpu as pltpu
from jax.sharding import PartitionSpec as P

NC = 8192
relaxation = 0.8
WEIGHT = relaxation / 6.0
CELL = 4
HALO = 4
F32 = jnp.float32
BF16 = jnp.bfloat16
MESH = pl.DeviceIdType.MESH
VMEM = pltpu.VMEM


def vmem_spec():
    return pl.BlockSpec(memory_space=pltpu.VMEM)


def any_spec():
    return pl.BlockSpec(memory_space=pl.ANY)


def params(**kw):
    return pltpu.CompilerParams(vmem_limit_bytes=60 * 1024 * 1024, **kw)


def pieces(value):
    hi = value.astype(BF16)
    rest = value - hi.astype(F32)
    mid = rest.astype(BF16)
    low = (rest - mid.astype(F32)).astype(BF16)
    return jnp.concatenate([hi, mid, low], axis=0)


def joined(value):
    k = value.shape[0] // 3
    return value[:k] + (value[k : 2 * k] + value[2 * k :])


def sweep(src, x0, x1, y0, y1, emit):
    Z = src.shape[-1]
    lane = lax.broadcasted_iota(jnp.int32, (src.shape[2], Z), 1)
    first, last = lane == 0, lane == Z - 1

    @pl.loop(x0, x1)
    def _(x):
        prev, here = src[x, y0 - 1], src[x, y0]
        for y in range(y0, y1):
            after = src[x, y + 1]
            near = src[x - 1, y] + src[x + 1, y] + (prev + after)
            low = jnp.where(first, 0.0, pltpu.roll(here, 1, 1))
            high = jnp.where(last, 0.0, pltpu.roll(here, Z - 1, 1))
            emit(x, y, here, near + (low + high))
            prev, here = here, after


def clear_outside(ref, G, M, X, Y, width):
    g, m = lax.axis_index("grp"), lax.axis_index("mem")
    h = HALO
    rest = ref.shape[2:]

    def rows(start):
        @pl.loop(start, start + width)
        def _(x):
            ref[x] = jnp.zeros(ref.shape[1:], F32)

    def columns(start):
        @pl.loop(h - width, h + X + width)
        def _(x):
            ref[x, start : start + width] = jnp.zeros((width,) + rest, F32)

    pl.when(g == 0)(lambda: rows(h - width))
    pl.when(g == G - 1)(lambda: rows(h + X))
    pl.when(m == 0)(lambda: columns(h - width))
    pl.when(m == M - 1)(lambda: columns(h + Y))


def down_kernel(
    G, M, n_own, f_hbm, a_ref, fac_hbm, fe_out, s3_out, ae, x_ref,
    f_ref, fe, s3, s2, res, means, hot, d_ref, r, pair, e, fac_ref,
    sx, rx, sy, ry, sc, rc, local, psend, precv, ssend, srecv, gsend, grecv, fsend, frecv,
):
    K, X, Y, Z = f_ref.shape
    Xe, Ye = X + 2 * HALO, Y + 2 * HALO
    bx, by, bz = a_ref.shape
    w = WEIGHT
    n = G * M // 2
    side = n_own // 2
    held = side * M
    g, m = lax.axis_index("grp"), lax.axis_index("mem")
    core = lax.rem(g, 2)
    me = (g // 2) * M + m
    own = m * side + g // 2
    q, bs = fac_ref.shape[0], fac_ref.shape[1]
    chunk = q * bs
    everyone = n_own == G
    partner = {"grp": g + 1 - 2 * core, "mem": m}
    flat = f_ref.reshape(K * X * Y, Z)

    def device(i):
        return {"grp": 2 * (i // M) + core, "mem": i % M}

    def peer(t):
        return lax.rem(me + t, n)

    def send(src, dst, ssem, rsem, to):
        return pltpu.make_async_remote_copy(
            src_ref=src, dst_ref=dst, send_sem=ssem, recv_sem=rsem, device_id=to, device_id_type=MESH
        )

    load = pltpu.make_async_copy(f_hbm, f_ref, local.at[3])
    load.start()
    barrier = pltpu.get_barrier_semaphore()

    def greet(to):
        pl.semaphore_signal(barrier, inc=1, device_id=to, device_id_type=MESH)

    greet(partner)
    pl.when(jnp.logical_and(core == 0, g > 0))(lambda: greet({"grp": g - 1, "mem": m}))
    pl.when(jnp.logical_and(core == 1, g < G - 1))(lambda: greet({"grp": g + 1, "mem": m}))

    @pl.loop(1, n)
    def _(t):
        greet(device(peer(t)))

    first = lax.rem(g, n_own) * q
    fetch = pltpu.make_async_copy(fac_hbm.at[pl.ds(first, q)], fac_ref, local.at[0])
    fetch.start()
    load.wait()

    @pl.loop(0, X)
    def _(x):
        for y in range(Y):
            fe[HALO + x, HALO + y] = flat[pl.ds(x * Y + y, K, stride=X * Y), :]

    for i in range(bx):
        for j in range(by):
            row = a_ref[i, j : j + 1, :]
            wide = jnp.concatenate([row] * (Z // bz), axis=1)
            ae[1 + i, 1 + j] = jnp.broadcast_to(wide, ae.shape[2:])

    def blank(start):
        @pl.loop(start, start + HALO)
        def _(x):
            fe[x, HALO : HALO + Y] = jnp.zeros((Y,) + fe.shape[2:], F32)

    def blank_side(start):
        @pl.loop(0, Xe)
        def _(x):
            fe[x, start : start + HALO] = jnp.zeros((HALO,) + fe.shape[2:], F32)

    @pl.when(g == 0)
    def _():
        blank(0)
        ae[0:1, 1 : 1 + by] = jnp.zeros((1, by) + ae.shape[2:], jnp.int32)

    @pl.when(g == G - 1)
    def _():
        blank(HALO + X)
        ae[1 + bx :, 1 : 1 + by] = jnp.zeros((1, by) + ae.shape[2:], jnp.int32)

    @pl.when(m == 0)
    def _():
        blank_side(0)
        ae[:, 0:1] = jnp.zeros((bx + 2, 1) + ae.shape[2:], jnp.int32)

    @pl.when(m == M - 1)
    def _():
        blank_side(HALO + Y)
        ae[:, 1 + by :] = jnp.zeros((bx + 2, 1) + ae.shape[2:], jnp.int32)

    pl.semaphore_wait(barrier, n + (g + G - 1) // G + (2 * (G - 1) - g) // G - 1)

    def copy(ref, src, dst, dev, sems, slot):
        return pltpu.make_async_remote_copy(
            src_ref=ref.at[src],
            dst_ref=ref.at[dst],
            send_sem=sems[0].at[slot],
            recv_sem=sems[1].at[slot],
            device_id=dev,
            device_id_type=MESH,
        )

    near = HALO - 1

    def across_axis(axis, d):
        whole = pl.ds(HALO, (Y, X)[axis])
        return (d, whole) if axis == 0 else (whole, d)

    def faces(down, axis, dev):
        n, nb, other = ((X, bx, by), (Y, by, bx))[axis]
        sems = (sx, rx) if axis == 0 else (sy, ry)
        base = 0 if down else 2
        src = pl.ds(HALO if down else HALO + n - near, near)
        dst = pl.ds(HALO + n if down else HALO - near, near)
        out = [copy(fe, across_axis(axis, src), across_axis(axis, dst), dev, sems, base)]
        src, dst = pl.ds(1 if down else nb, 1), pl.ds(1 + nb if down else 0, 1)
        whole = pl.ds(1, other)
        order = (lambda d: (d, whole)) if axis == 0 else (lambda d: (whole, d))
        return out + [copy(ae, order(src), order(dst), dev, sems, base + 1)]

    def far_faces(down, axis, dev):
        n = (X, Y)[axis]
        sems = (sx, rx) if axis == 0 else (sy, ry)
        src = pl.ds(HALO + near if down else n, 1)
        dst = pl.ds(HALO + n + near if down else 0, 1)
        return [copy(fe, across_axis(axis, src), across_axis(axis, dst), dev, sems, 4 if down else 5)]

    def corners(down, dev):
        out = []
        slot = 0 if down else 4 * HALO
        for d in range(1, near):
            width = near - d
            src = pl.ds(HALO if down else HALO + Y - width, width)
            dst = pl.ds(HALO + Y if down else HALO - width, width)
            for row in (HALO - d, HALO + X - 1 + d):
                out.append(copy(fe, (row, src), (row, dst), dev, (sc, rc), slot))
                slot += 1
        src = pl.ds(1 if down else by, 1)
        dst = pl.ds(1 + by if down else 0, 1)
        for row in (0, bx + 1):
            out.append(copy(ae, (row, src), (row, dst), dev, (sc, rc), slot))
            slot += 1
        return out

    def far_corners(down, dev):
        out = []
        slot = (0 if down else 4 * HALO) + 2 * HALO
        for d in range(1, HALO):
            layer = HALO - d
            src = pl.ds(HALO + layer - 1 if down else HALO + Y - layer, 1)
            dst = pl.ds(HALO + Y + layer - 1 if down else HALO - layer, 1)
            for row in (HALO - d, HALO + X - 1 + d):
                out.append(copy(fe, (row, src), (row, dst), dev, (sc, rc), slot))
                slot += 1
        return out

    def each(index, count, name, body):
        if count > 1:
            pl.when(index > 0)(lambda: body(True, {name: index - 1}))
            pl.when(index < count - 1)(lambda: body(False, {name: index + 1}))

    def begin(make):
        def body(down, dev):
            for c in make(down, dev):
                c.start()

        return body

    def end(make):
        def body(down, dev):
            for c in make(down, dev):
                c.wait_send()
            for c in make(not down, dev):
                c.wait_recv()

        return body

    def along(make, axis):
        return lambda down, dev: make(down, axis, dev)

    each(g, G, "grp", begin(along(faces, 0)))
    each(m, M, "mem", begin(along(faces, 1)))


    def second(x, y, c, near):
        s2[x, y] = w * ((2.0 - 6.0 * w) * c + w * near)

    def third(x, y, c, near):
        s3[x, y] = (1.0 - 6.0 * w) * c + w * (fe[x, y] + near)

    def residual(x, y, c, near):
        res[x - HALO, y - HALO] = fe[x, y] - 6.0 * c + near

    def inner(src, depth, emit):
        lo = HALO + depth
        sweep(src, lo, HALO + X - depth, lo, HALO + Y - depth, emit)

    def halo_row(src, d, y0, y1, emit):
        for x in (HALO - d, HALO + X - 1 + d):
            sweep(src, x, x + 1, y0, y1, emit)

    def ring(src, depth, reach, emit):
        lo, hx, hy = HALO + depth, HALO + X - depth, HALO + Y - depth
        y0, y1 = HALO - reach, HALO + Y + reach
        sweep(src, HALO, lo, y0, y1, emit)
        sweep(src, hx, HALO + X, y0, y1, emit)
        sweep(src, lo, hx, y0, lo, emit)
        sweep(src, lo, hx, hy, y1, emit)
        for d in range(1, reach + 1):
            halo_row(src, d, y0 + d, y1 - d, emit)

    def frame(src, reach, emit):
        y0, y1 = HALO - reach, HALO + Y + reach
        sweep(src, HALO, HALO + X, y0, y0 + 1, emit)
        sweep(src, HALO, HALO + X, y1 - 1, y1, emit)
        for d in range(1, reach):
            halo_row(src, d, y0 + d, y0 + d + 1, emit)
            halo_row(src, d, y1 - d - 1, y1 - d, emit)
        halo_row(src, reach, HALO, HALO + Y, emit)

    inner(fe, 1, second)
    inner(s2, 2, third)

    count = bx * by * bz
    ids = jnp.concatenate(
        [a_ref[i, j : j + 1, :] for i in range(bx) for j in range(by)], axis=1
    )
    entry = lax.broadcasted_iota(jnp.int32, (chunk, count), 0)

    def owner_of(c, h):
        return (h // side) * 2 * side + 2 * (h % side) + c

    @pl.loop(0, held)
    def _(h):
        for c in range(2):
            hit = entry == ids - owner_of(c, h) * chunk
            hot[c, h] = jnp.where(hit, 1.0, 0.0).astype(BF16)

    each(g, G, "grp", end(along(faces, 0)))
    each(m, M, "mem", begin(corners))
    each(m, M, "mem", end(along(faces, 1)))
    each(g, G, "grp", begin(along(far_faces, 0)))
    each(m, M, "mem", begin(along(far_faces, 1)))
    each(m, M, "mem", end(corners))
    each(m, M, "mem", begin(far_corners))

    ring(fe, 1, 2, second)
    clear_outside(s2, G, M, X, Y, 2)
    ring(s2, 2, 1, third)
    clear_outside(s3, G, M, X, Y, 1)
    inner(s3, 0, residual)

    rows = lax.broadcasted_iota(jnp.int32, (by * Z, by * bz), 0)
    cols = lax.broadcasted_iota(jnp.int32, (by * Z, by * bz), 1)
    spread = jnp.where(rows // CELL == cols, 1.0 / CELL**3, 0.0).astype(BF16)
    for i in range(bx):
        parts = []
        for j in range(by):
            total = None
            for p in range(CELL):
                for t in range(CELL):
                    v = res[i * CELL + p, j * CELL + t]
                    total = v if total is None else total + v
            parts.append(total)
        line = jnp.concatenate(parts, axis=1)
        means[:, i * by * bz : (i + 1) * by * bz] = joined(
            jnp.dot(pieces(line), spread, preferred_element_type=F32)
        )
    split = pieces(means[...])

    def scatter(c):
        @pl.loop(0, held)
        def _(h):
            got = lax.dot_general(
                split, hot[c, h], (((1,), (1,)), ((), ())), preferred_element_type=F32
            )
            d_ref[c, h] = joined(got)

    scatter(1 - core)
    def owning(i, body):
        if everyone:
            body()
        else:
            pl.when(i // M < side)(body)

    swap = send(d_ref.at[1 - core], pair, psend, precv, partner)
    swap.start()
    scatter(core)
    swap.wait()

    @pl.loop(0, held)
    def _(h):
        e[h] = d_ref[core, h] + pair[h]

    @pl.loop(1, n)
    def _(t):
        to = peer(t)
        block = (to % M) * side + to // M
        owning(to, lambda: send(e.at[block], r.at[me], ssend, srecv, device(to)).start())

    def wait_bytes(ref, count, sem):
        if count > 0:
            part = ref.at[pl.ds(0, count)]
            pltpu.make_async_copy(part, part, sem).wait()


    each(g, G, "grp", end(along(far_faces, 0)))
    each(m, M, "mem", end(along(far_faces, 1)))
    each(m, M, "mem", end(far_corners))
    fe_copy = pltpu.make_async_copy(
        fe.at[pl.ds(HALO - 1, X + 2), pl.ds(HALO - 1, Y + 2)], fe_out, local.at[1]
    )
    fe_copy.start()
    frame(fe, 3, second)
    clear_outside(s2, G, M, X, Y, 3)
    frame(s2, 2, third)
    clear_outside(s3, G, M, X, Y, 2)
    s3_copy = pltpu.make_async_copy(
        s3.at[pl.ds(HALO - 2, X + 4), pl.ds(HALO - 2, Y + 4)], s3_out, local.at[2]
    )
    s3_copy.start()
    fetch.wait()

    def solve():
        wait_bytes(r, n - 1, srecv)

        def add(t, total):
            return total + r[peer(t)]

        total = lax.fori_loop(1, n, add, e[own])
        for b in range(q):
            rhs = total[:, b * bs : (b + 1) * bs]
            inner = lax.dot_general(
                rhs,
                fac_ref[b],
                (((1,), (1,)), ((), ())),
                precision=lax.Precision.HIGHEST,
                preferred_element_type=F32,
            )
            x_ref[core, own, :, b * bs : (b + 1) * bs] = lax.dot_general(
                inner,
                fac_ref[b],
                (((1,), (0,)), ((), ())),
                precision=lax.Precision.HIGHEST,
                preferred_element_type=F32,
            )

        @pl.loop(1, n)
        def _(t):
            mine = x_ref.at[core, own]
            send(mine, mine, gsend, grecv, device(peer(t))).start()

    owning(me, solve)

    if everyone:
        wait_bytes(e, held - 1, ssend)
        wait_bytes(e, held - 1, grecv)
        wait_bytes(r, n - 1, gsend)
    else:
        mine = g < n_own

        @pl.when(mine)
        def _():
            wait_bytes(e, held - 1, ssend)
            wait_bytes(e, held - 1, grecv)
            wait_bytes(r, n - 1, gsend)

        @pl.when(jnp.logical_not(mine))
        def _():
            wait_bytes(e, held, ssend)
            wait_bytes(e, held, grecv)

    forward = send(x_ref.at[core], x_ref.at[core], fsend, frecv, partner)
    forward.start()
    forward.wait()
    fe_copy.wait()
    s3_copy.wait()


def post_kernel(G, M, bs, side, fe_hbm, s3_hbm, ae, x_ref, o_hbm, lifted, sol, fe, s3, o_ref, sems):
    Xe, Ye, K, Z = fe.shape
    X, Y = Xe - 2 * HALO, Ye - 2 * HALO
    bx, by, bz = X // CELL + 2, Y // CELL + 2, Z // CELL
    loads = [
        pltpu.make_async_copy(s3_hbm, s3.at[pl.ds(HALO - 2, X + 4), pl.ds(HALO - 2, Y + 4)], sems.at[0]),
        pltpu.make_async_copy(fe_hbm, fe.at[pl.ds(HALO - 1, X + 2), pl.ds(HALO - 1, Y + 2)], sems.at[1]),
    ]
    for c in loads:
        c.start()
    w = WEIGHT
    half = 8
    q = x_ref.shape[3] // bs
    per = Z // bz
    groups = [range(s, min(s + per, by)) for s in range(0, by, per)]
    lane = lax.broadcasted_iota(jnp.int32, (half, Z), 1)

    def pick(table, index):
        return jnp.take_along_axis(table, index, axis=1)

    def lines(base, count):
        rows = [(base + d, group) for d in range(count) for group in groups]
        inner, outer = [], []
        for i, group in rows:
            index = None
            for slot, j in enumerate(group):
                packed = ae[i, j]
                index = packed if index is None else jnp.where(lane // bz == slot, packed, index)
            inner.append(index % bs)
            outer.append(index // bs)
        halves = K // half

        def body(h, found):
            out = list(found)
            for c in range(2):
                owner = (h // side) * 2 * side + 2 * (h % side) + c
                for b in range(q):
                    tables = [
                        x_ref[c, h, t * half : (t + 1) * half, b * bs : (b + 1) * bs]
                        for t in range(halves)
                    ]
                    for e in range(len(rows)):
                        hit = outer[e] == owner * q + b
                        for t in range(halves):
                            k = e * halves + t
                            out[k] = jnp.where(hit, pick(tables[t], inner[e]), out[k])
            return tuple(out)

        zeros = tuple(jnp.zeros((half, Z), F32) for _ in range(len(rows) * halves))
        found = lax.fori_loop(0, x_ref.shape[1], body, zeros)
        for e, (i, group) in enumerate(rows):
            for slot, j in enumerate(group):
                wide = [
                    pick(found[e * halves + t], lane // CELL + slot * bz) for t in range(halves)
                ]
                value = jnp.concatenate(wide, axis=0)
                for p in range(CELL):
                    for r in range(CELL):
                        lifted[i * CELL + p, j * CELL + r] = value

    batch = max(d for d in (1, 2, 3) if bx % d == 0)

    @pl.loop(0, bx // batch)
    def _(i):
        lines(i * batch, batch)

    clear_outside(lifted, G, M, X, Y, HALO)
    loads[0].wait()

    def start(x, y, c, near):
        sol[x, y] = s3[x, y] + ((1.0 - 6.0 * w) * c + w * near)

    sweep(lifted, 2, Xe - 2, 2, Ye - 2, start)
    clear_outside(sol, G, M, X, Y, 2)
    loads[1].wait()

    def first(x, y, c, near):
        lifted[x, y] = (1.0 - 6.0 * w) * c + w * (fe[x, y] + near)

    sweep(sol, 3, Xe - 3, 3, Ye - 3, first)
    clear_outside(lifted, G, M, X, Y, 1)

    flat = o_ref.reshape(K * X * Y, Z)

    def last(x, y, c, near):
        flat[pl.ds((x - HALO) * Y + (y - HALO), K, stride=X * Y), :] = (
            1.0 - 6.0 * w
        ) * c + w * (fe[x, y] + near)

    step = X // CELL
    stores = []
    for i in range(CELL):
        sweep(lifted, HALO + i * step, HALO + (i + 1) * step, HALO, HALO + Y, last)
        part = pl.ds(i * step, step)
        stores.append(pltpu.make_async_copy(o_ref.at[:, part], o_hbm.at[:, part], sems.at[2 + i]))
        stores[-1].start()
    for c in stores:
        c.wait()


def shards(G, M, forcing, aggregate, factors):
    K, X, Y, Z = forcing.shape
    bx, by, bz = aggregate.shape
    Xe, Ye = X + 2 * HALO, Y + 2 * HALO
    local_blocks, bs = factors.shape[0], factors.shape[1]
    q = -(-local_blocks // G)
    n_own = local_blocks // q
    chunk = q * bs
    owners = n_own * M
    sd = jax.ShapeDtypeStruct

    fe, s3, ae, fix = pl.pallas_call(
        functools.partial(down_kernel, G, M, n_own),
        out_shape=(
            sd((X + 2, Y + 2, K, Z), F32),
            sd((X + 4, Y + 4, K, Z), F32),
            sd((bx + 2, by + 2, 8, Z), jnp.int32),
            sd((2, owners // 2, K, chunk), F32),
        ),
        in_specs=[any_spec(), vmem_spec(), any_spec()],
        out_specs=(any_spec(), any_spec(), vmem_spec(), vmem_spec()),
        scratch_shapes=[VMEM((K, X, Y, Z), F32)]
        + [VMEM((Xe, Ye, K, Z), F32)] * 3
        + [
            VMEM((X, Y, K, Z), F32),
            VMEM((K, bx * by * bz), F32),
            VMEM((2, owners // 2, chunk, bx * by * bz), BF16),
            VMEM((2, owners // 2, K, chunk), F32),
            VMEM((G * M // 2, K, chunk), F32),
            VMEM((owners // 2, K, chunk), F32),
            VMEM((owners // 2, K, chunk), F32),
            VMEM((q, bs, bs), F32),
        ]
        + [pltpu.SemaphoreType.DMA((6,))] * 4
        + [pltpu.SemaphoreType.DMA((8 * HALO,))] * 2
        + [pltpu.SemaphoreType.DMA((4,))]
        + [pltpu.SemaphoreType.DMA] * 8,
        compiler_params=params(collective_id=0, has_side_effects=True),
        name="down",
    )(forcing, aggregate, factors)

    return pl.pallas_call(
        functools.partial(post_kernel, G, M, bs, n_own // 2),
        out_shape=sd((K, X, Y, Z), F32),
        in_specs=[any_spec(), any_spec(), vmem_spec(), vmem_spec()],
        out_specs=any_spec(),
        scratch_shapes=[VMEM((Xe, Ye, K, Z), F32)] * 4
        + [VMEM((K, X, Y, Z), F32), pltpu.SemaphoreType.DMA((2 + CELL,))],
        compiler_params=params(),
        name="post",
    )(fe, s3, ae, fix)


def solution(mesh):
    placed = (P(None, "grp", "mem", None), P("grp", "mem", None), P("mem", None, None))
    body = functools.partial(shards, mesh.shape["grp"], mesh.shape["mem"])
    return jax.shard_map(
        body, mesh=mesh, in_specs=placed, out_specs=P(None, "grp", "mem", None), check_vma=False
    )
```

```python
import functools

import jax
import jax.numpy as jnp
from jax import lax
from jax.experimental import pallas as pl
from jax.experimental.pallas import tpu as pltpu
from jax.sharding import PartitionSpec as P

NC = 8192
relaxation = 0.8
WEIGHT = relaxation / 6.0
CELL = 4
HALO = 4
F32 = jnp.float32
BF16 = jnp.bfloat16
MESH = pl.DeviceIdType.MESH
VMEM = pltpu.VMEM


def vmem_spec():
    return pl.BlockSpec(memory_space=pltpu.VMEM)


def any_spec():
    return pl.BlockSpec(memory_space=pl.ANY)


def params(**kw):
    return pltpu.CompilerParams(vmem_limit_bytes=60 * 1024 * 1024, **kw)


def pieces(value):
    hi = value.astype(BF16)
    rest = value - hi.astype(F32)
    mid = rest.astype(BF16)
    low = (rest - mid.astype(F32)).astype(BF16)
    return jnp.concatenate([hi, mid, low], axis=0)


def joined(value):
    k = value.shape[0] // 3
    return value[:k] + (value[k : 2 * k] + value[2 * k :])


def sweep(src, x0, x1, y0, y1, emit):
    Z = src.shape[-1]
    lane = lax.broadcasted_iota(jnp.int32, (src.shape[2], Z), 1)
    first, last = lane == 0, lane == Z - 1

    @pl.loop(x0, x1)
    def _(x):
        prev, here = src[x, y0 - 1], src[x, y0]
        for y in range(y0, y1):
            after = src[x, y + 1]
            near = src[x - 1, y] + src[x + 1, y] + (prev + after)
            low = jnp.where(first, 0.0, pltpu.roll(here, 1, 1))
            high = jnp.where(last, 0.0, pltpu.roll(here, Z - 1, 1))
            emit(x, y, here, near + (low + high))
            prev, here = here, after


def clear_outside(ref, G, M, X, Y, width):
    g, m = lax.axis_index("grp"), lax.axis_index("mem")
    h = HALO
    rest = ref.shape[2:]

    def rows(start):
        @pl.loop(start, start + width)
        def _(x):
            ref[x] = jnp.zeros(ref.shape[1:], F32)

    def columns(start):
        @pl.loop(h - width, h + X + width)
        def _(x):
            ref[x, start : start + width] = jnp.zeros((width,) + rest, F32)

    pl.when(g == 0)(lambda: rows(h - width))
    pl.when(g == G - 1)(lambda: rows(h + X))
    pl.when(m == 0)(lambda: columns(h - width))
    pl.when(m == M - 1)(lambda: columns(h + Y))


def down_kernel(
    G, M, n_own, f_hbm, a_ref, fac_hbm, fe_out, s3_out, ae, x_ref,
    f_ref, fe, s3, s2, res, means, hot, d_ref, r, pair, e, fac_ref,
    sx, rx, sy, ry, sc, rc, local, psend, precv, ssend, srecv, gsend, grecv, fsend, frecv,
):
    K, X, Y, Z = f_ref.shape
    Xe, Ye = X + 2 * HALO, Y + 2 * HALO
    bx, by, bz = a_ref.shape
    w = WEIGHT
    n = G * M // 2
    side = n_own // 2
    held = side * M
    g, m = lax.axis_index("grp"), lax.axis_index("mem")
    core = lax.rem(g, 2)
    me = (g // 2) * M + m
    own = m * side + g // 2
    q, bs = fac_ref.shape[0], fac_ref.shape[1]
    chunk = q * bs
    everyone = n_own == G
    partner = {"grp": g + 1 - 2 * core, "mem": m}
    flat = f_ref.reshape(K * X * Y, Z)

    def device(i):
        return {"grp": 2 * (i // M) + core, "mem": i % M}

    def peer(t):
        return lax.rem(me + t, n)

    def send(src, dst, ssem, rsem, to):
        return pltpu.make_async_remote_copy(
            src_ref=src, dst_ref=dst, send_sem=ssem, recv_sem=rsem, device_id=to, device_id_type=MESH
        )

    load = pltpu.make_async_copy(f_hbm, f_ref, local.at[3])
    load.start()
    barrier = pltpu.get_barrier_semaphore()

    def greet(to):
        pl.semaphore_signal(barrier, inc=1, device_id=to, device_id_type=MESH)

    greet(partner)
    pl.when(jnp.logical_and(core == 0, g > 0))(lambda: greet({"grp": g - 1, "mem": m}))
    pl.when(jnp.logical_and(core == 1, g < G - 1))(lambda: greet({"grp": g + 1, "mem": m}))

    @pl.loop(1, n)
    def _(t):
        greet(device(peer(t)))

    first = lax.rem(g, n_own) * q
    fetch = pltpu.make_async_copy(fac_hbm.at[pl.ds(first, q)], fac_ref, local.at[0])
    fetch.start()
    load.wait()

    edge = HALO - 1

    def turn(x0, x1, columns):
        @pl.loop(x0, x1)
        def _(x):
            for y in columns:
                fe[HALO + x, HALO + y] = flat[pl.ds(x * Y + y, K, stride=X * Y), :]

    turn(0, edge, range(Y))
    turn(X - edge, X, range(Y))
    turn(edge, X - edge, [*range(edge), *range(Y - edge, Y)])

    for i in range(bx):
        for j in range(by):
            row = a_ref[i, j : j + 1, :]
            wide = jnp.concatenate([row] * (Z // bz), axis=1)
            ae[1 + i, 1 + j] = jnp.broadcast_to(wide, ae.shape[2:])

    def blank(start):
        @pl.loop(start, start + HALO)
        def _(x):
            fe[x, HALO : HALO + Y] = jnp.zeros((Y,) + fe.shape[2:], F32)

    def blank_side(start):
        @pl.loop(0, Xe)
        def _(x):
            fe[x, start : start + HALO] = jnp.zeros((HALO,) + fe.shape[2:], F32)

    @pl.when(g == 0)
    def _():
        blank(0)
        ae[0:1, 1 : 1 + by] = jnp.zeros((1, by) + ae.shape[2:], jnp.int32)

    @pl.when(g == G - 1)
    def _():
        blank(HALO + X)
        ae[1 + bx :, 1 : 1 + by] = jnp.zeros((1, by) + ae.shape[2:], jnp.int32)

    @pl.when(m == 0)
    def _():
        blank_side(0)
        ae[:, 0:1] = jnp.zeros((bx + 2, 1) + ae.shape[2:], jnp.int32)

    @pl.when(m == M - 1)
    def _():
        blank_side(HALO + Y)
        ae[:, 1 + by :] = jnp.zeros((bx + 2, 1) + ae.shape[2:], jnp.int32)

    pl.semaphore_wait(barrier, n + (g + G - 1) // G + (2 * (G - 1) - g) // G - 1)

    def copy(ref, src, dst, dev, sems, slot):
        return pltpu.make_async_remote_copy(
            src_ref=ref.at[src],
            dst_ref=ref.at[dst],
            send_sem=sems[0].at[slot],
            recv_sem=sems[1].at[slot],
            device_id=dev,
            device_id_type=MESH,
        )

    near = HALO - 1

    def across_axis(axis, d):
        whole = pl.ds(HALO, (Y, X)[axis])
        return (d, whole) if axis == 0 else (whole, d)

    def faces(down, axis, dev):
        n, nb, other = ((X, bx, by), (Y, by, bx))[axis]
        sems = (sx, rx) if axis == 0 else (sy, ry)
        base = 0 if down else 2
        src = pl.ds(HALO if down else HALO + n - near, near)
        dst = pl.ds(HALO + n if down else HALO - near, near)
        out = [copy(fe, across_axis(axis, src), across_axis(axis, dst), dev, sems, base)]
        src, dst = pl.ds(1 if down else nb, 1), pl.ds(1 + nb if down else 0, 1)
        whole = pl.ds(1, other)
        order = (lambda d: (d, whole)) if axis == 0 else (lambda d: (whole, d))
        return out + [copy(ae, order(src), order(dst), dev, sems, base + 1)]

    def far_faces(down, axis, dev):
        n = (X, Y)[axis]
        sems = (sx, rx) if axis == 0 else (sy, ry)
        src = pl.ds(HALO + near if down else n, 1)
        dst = pl.ds(HALO + n + near if down else 0, 1)
        return [copy(fe, across_axis(axis, src), across_axis(axis, dst), dev, sems, 4 if down else 5)]

    def corners(down, dev):
        out = []
        slot = 0 if down else 4 * HALO
        for d in range(1, near):
            width = near - d
            src = pl.ds(HALO if down else HALO + Y - width, width)
            dst = pl.ds(HALO + Y if down else HALO - width, width)
            for row in (HALO - d, HALO + X - 1 + d):
                out.append(copy(fe, (row, src), (row, dst), dev, (sc, rc), slot))
                slot += 1
        src = pl.ds(1 if down else by, 1)
        dst = pl.ds(1 + by if down else 0, 1)
        for row in (0, bx + 1):
            out.append(copy(ae, (row, src), (row, dst), dev, (sc, rc), slot))
            slot += 1
        return out

    def far_corners(down, dev):
        out = []
        slot = (0 if down else 4 * HALO) + 2 * HALO
        for d in range(1, HALO):
            layer = HALO - d
            src = pl.ds(HALO + layer - 1 if down else HALO + Y - layer, 1)
            dst = pl.ds(HALO + Y + layer - 1 if down else HALO - layer, 1)
            for row in (HALO - d, HALO + X - 1 + d):
                out.append(copy(fe, (row, src), (row, dst), dev, (sc, rc), slot))
                slot += 1
        return out

    def each(index, count, name, body):
        if count > 1:
            pl.when(index > 0)(lambda: body(True, {name: index - 1}))
            pl.when(index < count - 1)(lambda: body(False, {name: index + 1}))

    def begin(make):
        def body(down, dev):
            for c in make(down, dev):
                c.start()

        return body

    def end(make):
        def body(down, dev):
            for c in make(down, dev):
                c.wait_send()
            for c in make(not down, dev):
                c.wait_recv()

        return body

    def along(make, axis):
        return lambda down, dev: make(down, axis, dev)

    each(g, G, "grp", begin(along(faces, 0)))
    each(m, M, "mem", begin(along(faces, 1)))

    turn(edge, X - edge, range(edge, Y - edge))


    def second(x, y, c, near):
        s2[x, y] = w * ((2.0 - 6.0 * w) * c + w * near)

    def third(x, y, c, near):
        s3[x, y] = (1.0 - 6.0 * w) * c + w * (fe[x, y] + near)

    def residual(x, y, c, near):
        res[x - HALO, y - HALO] = fe[x, y] - 6.0 * c + near

    def inner(src, depth, emit):
        lo = HALO + depth
        sweep(src, lo, HALO + X - depth, lo, HALO + Y - depth, emit)

    def halo_row(src, d, y0, y1, emit):
        for x in (HALO - d, HALO + X - 1 + d):
            sweep(src, x, x + 1, y0, y1, emit)

    def ring(src, depth, reach, emit):
        lo, hx, hy = HALO + depth, HALO + X - depth, HALO + Y - depth
        y0, y1 = HALO - reach, HALO + Y + reach
        sweep(src, HALO, lo, y0, y1, emit)
        sweep(src, hx, HALO + X, y0, y1, emit)
        sweep(src, lo, hx, y0, lo, emit)
        sweep(src, lo, hx, hy, y1, emit)
        for d in range(1, reach + 1):
            halo_row(src, d, y0 + d, y1 - d, emit)

    def frame(src, reach, emit):
        y0, y1 = HALO - reach, HALO + Y + reach
        sweep(src, HALO, HALO + X, y0, y0 + 1, emit)
        sweep(src, HALO, HALO + X, y1 - 1, y1, emit)
        for d in range(1, reach):
            halo_row(src, d, y0 + d, y0 + d + 1, emit)
            halo_row(src, d, y1 - d - 1, y1 - d, emit)
        halo_row(src, reach, HALO, HALO + Y, emit)

    inner(fe, 1, second)
    inner(s2, 2, third)

    count = bx * by * bz
    ids = jnp.concatenate(
        [a_ref[i, j : j + 1, :] for i in range(bx) for j in range(by)], axis=1
    )
    entry = lax.broadcasted_iota(jnp.int32, (chunk, count), 0)

    def owner_of(c, h):
        return (h // side) * 2 * side + 2 * (h % side) + c

    @pl.loop(0, held)
    def _(h):
        for c in range(2):
            hit = entry == ids - owner_of(c, h) * chunk
            hot[c, h] = jnp.where(hit, 1.0, 0.0).astype(BF16)

    each(g, G, "grp", end(along(faces, 0)))
    each(m, M, "mem", begin(corners))
    each(m, M, "mem", end(along(faces, 1)))
    each(g, G, "grp", begin(along(far_faces, 0)))
    each(m, M, "mem", begin(along(far_faces, 1)))
    each(m, M, "mem", end(corners))
    each(m, M, "mem", begin(far_corners))

    ring(fe, 1, 2, second)
    clear_outside(s2, G, M, X, Y, 2)
    ring(s2, 2, 1, third)
    clear_outside(s3, G, M, X, Y, 1)
    inner(s3, 0, residual)

    rows = lax.broadcasted_iota(jnp.int32, (by * Z, by * bz), 0)
    cols = lax.broadcasted_iota(jnp.int32, (by * Z, by * bz), 1)
    spread = jnp.where(rows // CELL == cols, 1.0 / CELL**3, 0.0).astype(BF16)
    for i in range(bx):
        parts = []
        for j in range(by):
            total = None
            for p in range(CELL):
                for t in range(CELL):
                    v = res[i * CELL + p, j * CELL + t]
                    total = v if total is None else total + v
            parts.append(total)
        line = jnp.concatenate(parts, axis=1)
        means[:, i * by * bz : (i + 1) * by * bz] = joined(
            jnp.dot(pieces(line), spread, preferred_element_type=F32)
        )
    split = pieces(means[...])

    def scatter(c):
        @pl.loop(0, held)
        def _(h):
            got = lax.dot_general(
                split, hot[c, h], (((1,), (1,)), ((), ())), preferred_element_type=F32
            )
            d_ref[c, h] = joined(got)

    scatter(1 - core)
    def owning(i, body):
        if everyone:
            body()
        else:
            pl.when(i // M < side)(body)

    swap = send(d_ref.at[1 - core], pair, psend, precv, partner)
    swap.start()
    scatter(core)
    swap.wait()

    @pl.loop(0, held)
    def _(h):
        e[h] = d_ref[core, h] + pair[h]

    @pl.loop(1, n)
    def _(t):
        to = peer(t)
        block = (to % M) * side + to // M
        owning(to, lambda: send(e.at[block], r.at[me], ssend, srecv, device(to)).start())

    def wait_bytes(ref, count, sem):
        if count > 0:
            part = ref.at[pl.ds(0, count)]
            pltpu.make_async_copy(part, part, sem).wait()


    each(g, G, "grp", end(along(far_faces, 0)))
    each(m, M, "mem", end(along(far_faces, 1)))
    each(m, M, "mem", end(far_corners))
    fe_copy = pltpu.make_async_copy(
        fe.at[pl.ds(HALO - 1, X + 2), pl.ds(HALO - 1, Y + 2)], fe_out, local.at[1]
    )
    fe_copy.start()
    frame(fe, 3, second)
    clear_outside(s2, G, M, X, Y, 3)
    frame(s2, 2, third)
    clear_outside(s3, G, M, X, Y, 2)
    s3_copy = pltpu.make_async_copy(
        s3.at[pl.ds(HALO - 2, X + 4), pl.ds(HALO - 2, Y + 4)], s3_out, local.at[2]
    )
    s3_copy.start()
    fetch.wait()

    def solve():
        wait_bytes(r, n - 1, srecv)

        def add(t, total):
            return total + r[peer(t)]

        total = lax.fori_loop(1, n, add, e[own])
        for b in range(q):
            rhs = total[:, b * bs : (b + 1) * bs]
            inner = lax.dot_general(
                rhs,
                fac_ref[b],
                (((1,), (1,)), ((), ())),
                precision=lax.Precision.HIGHEST,
                preferred_element_type=F32,
            )
            x_ref[core, own, :, b * bs : (b + 1) * bs] = lax.dot_general(
                inner,
                fac_ref[b],
                (((1,), (0,)), ((), ())),
                precision=lax.Precision.HIGHEST,
                preferred_element_type=F32,
            )

        @pl.loop(1, n)
        def _(t):
            mine = x_ref.at[core, own]
            send(mine, mine, gsend, grecv, device(peer(t))).start()

    owning(me, solve)

    if everyone:
        wait_bytes(e, held - 1, ssend)
        wait_bytes(e, held - 1, grecv)
        wait_bytes(r, n - 1, gsend)
    else:
        mine = g < n_own

        @pl.when(mine)
        def _():
            wait_bytes(e, held - 1, ssend)
            wait_bytes(e, held - 1, grecv)
            wait_bytes(r, n - 1, gsend)

        @pl.when(jnp.logical_not(mine))
        def _():
            wait_bytes(e, held, ssend)
            wait_bytes(e, held, grecv)

    forward = send(x_ref.at[core], x_ref.at[core], fsend, frecv, partner)
    forward.start()
    forward.wait()
    fe_copy.wait()
    s3_copy.wait()


def post_kernel(G, M, bs, side, fe_hbm, s3_hbm, ae, x_ref, o_hbm, lifted, sol, fe, s3, o_ref, sems):
    Xe, Ye, K, Z = fe.shape
    X, Y = Xe - 2 * HALO, Ye - 2 * HALO
    bx, by, bz = X // CELL + 2, Y // CELL + 2, Z // CELL
    loads = [
        pltpu.make_async_copy(s3_hbm, s3.at[pl.ds(HALO - 2, X + 4), pl.ds(HALO - 2, Y + 4)], sems.at[0]),
        pltpu.make_async_copy(fe_hbm, fe.at[pl.ds(HALO - 1, X + 2), pl.ds(HALO - 1, Y + 2)], sems.at[1]),
    ]
    for c in loads:
        c.start()
    w = WEIGHT
    half = 8
    q = x_ref.shape[3] // bs
    per = Z // bz
    groups = [range(s, min(s + per, by)) for s in range(0, by, per)]
    lane = lax.broadcasted_iota(jnp.int32, (half, Z), 1)

    def pick(table, index):
        return jnp.take_along_axis(table, index, axis=1)

    def lines(base, count):
        rows = [(base + d, group) for d in range(count) for group in groups]
        inner, outer = [], []
        for i, group in rows:
            index = None
            for slot, j in enumerate(group):
                packed = ae[i, j]
                index = packed if index is None else jnp.where(lane // bz == slot, packed, index)
            inner.append(index % bs)
            outer.append(index // bs)
        halves = K // half

        def body(h, found):
            out = list(found)
            for c in range(2):
                owner = (h // side) * 2 * side + 2 * (h % side) + c
                for b in range(q):
                    tables = [
                        x_ref[c, h, t * half : (t + 1) * half, b * bs : (b + 1) * bs]
                        for t in range(halves)
                    ]
                    for e in range(len(rows)):
                        hit = outer[e] == owner * q + b
                        for t in range(halves):
                            k = e * halves + t
                            out[k] = jnp.where(hit, pick(tables[t], inner[e]), out[k])
            return tuple(out)

        zeros = tuple(jnp.zeros((half, Z), F32) for _ in range(len(rows) * halves))
        found = lax.fori_loop(0, x_ref.shape[1], body, zeros)
        for e, (i, group) in enumerate(rows):
            for slot, j in enumerate(group):
                wide = [
                    pick(found[e * halves + t], lane // CELL + slot * bz) for t in range(halves)
                ]
                value = jnp.concatenate(wide, axis=0)
                for p in range(CELL):
                    for r in range(CELL):
                        lifted[i * CELL + p, j * CELL + r] = value

    batch = max(d for d in (1, 2, 3) if bx % d == 0)

    @pl.loop(0, bx // batch)
    def _(i):
        lines(i * batch, batch)

    clear_outside(lifted, G, M, X, Y, HALO)
    loads[0].wait()

    def start(x, y, c, near):
        sol[x, y] = s3[x, y] + ((1.0 - 6.0 * w) * c + w * near)

    sweep(lifted, 2, Xe - 2, 2, Ye - 2, start)
    clear_outside(sol, G, M, X, Y, 2)
    loads[1].wait()

    def first(x, y, c, near):
        lifted[x, y] = (1.0 - 6.0 * w) * c + w * (fe[x, y] + near)

    sweep(sol, 3, Xe - 3, 3, Ye - 3, first)
    clear_outside(lifted, G, M, X, Y, 1)

    flat = o_ref.reshape(K * X * Y, Z)

    def last(x, y, c, near):
        flat[pl.ds((x - HALO) * Y + (y - HALO), K, stride=X * Y), :] = (
            1.0 - 6.0 * w
        ) * c + w * (fe[x, y] + near)

    step = X // CELL
    stores = []
    for i in range(CELL):
        sweep(lifted, HALO + i * step, HALO + (i + 1) * step, HALO, HALO + Y, last)
        part = pl.ds(i * step, step)
        stores.append(pltpu.make_async_copy(o_ref.at[:, part], o_hbm.at[:, part], sems.at[2 + i]))
        stores[-1].start()
    for c in stores:
        c.wait()


def shards(G, M, forcing, aggregate, factors):
    K, X, Y, Z = forcing.shape
    bx, by, bz = aggregate.shape
    Xe, Ye = X + 2 * HALO, Y + 2 * HALO
    local_blocks, bs = factors.shape[0], factors.shape[1]
    q = -(-local_blocks // G)
    n_own = local_blocks // q
    chunk = q * bs
    owners = n_own * M
    sd = jax.ShapeDtypeStruct

    fe, s3, ae, fix = pl.pallas_call(
        functools.partial(down_kernel, G, M, n_own),
        out_shape=(
            sd((X + 2, Y + 2, K, Z), F32),
            sd((X + 4, Y + 4, K, Z), F32),
            sd((bx + 2, by + 2, 8, Z), jnp.int32),
            sd((2, owners // 2, K, chunk), F32),
        ),
        in_specs=[any_spec(), vmem_spec(), any_spec()],
        out_specs=(any_spec(), any_spec(), vmem_spec(), vmem_spec()),
        scratch_shapes=[VMEM((K, X, Y, Z), F32)]
        + [VMEM((Xe, Ye, K, Z), F32)] * 3
        + [
            VMEM((X, Y, K, Z), F32),
            VMEM((K, bx * by * bz), F32),
            VMEM((2, owners // 2, chunk, bx * by * bz), BF16),
            VMEM((2, owners // 2, K, chunk), F32),
            VMEM((G * M // 2, K, chunk), F32),
            VMEM((owners // 2, K, chunk), F32),
            VMEM((owners // 2, K, chunk), F32),
            VMEM((q, bs, bs), F32),
        ]
        + [pltpu.SemaphoreType.DMA((6,))] * 4
        + [pltpu.SemaphoreType.DMA((8 * HALO,))] * 2
        + [pltpu.SemaphoreType.DMA((4,))]
        + [pltpu.SemaphoreType.DMA] * 8,
        compiler_params=params(collective_id=0, has_side_effects=True),
        name="down",
    )(forcing, aggregate, factors)

    return pl.pallas_call(
        functools.partial(post_kernel, G, M, bs, n_own // 2),
        out_shape=sd((K, X, Y, Z), F32),
        in_specs=[any_spec(), any_spec(), vmem_spec(), vmem_spec()],
        out_specs=any_spec(),
        scratch_shapes=[VMEM((Xe, Ye, K, Z), F32)] * 4
        + [VMEM((K, X, Y, Z), F32), pltpu.SemaphoreType.DMA((2 + CELL,))],
        compiler_params=params(),
        name="post",
    )(fe, s3, ae, fix)


def solution(mesh):
    placed = (P(None, "grp", "mem", None), P("grp", "mem", None), P("mem", None, None))
    body = functools.partial(shards, mesh.shape["grp"], mesh.shape["mem"])
    return jax.shard_map(
        body, mesh=mesh, in_specs=placed, out_specs=P(None, "grp", "mem", None), check_vma=False
    )
```
